512 devices in a mesh: grp: 8 (over x, core), ep: 64 (over z, y).
Axes of the slice: x: 4, y: 8, z: 8, core: 2. Of those that a mesh axis runs over, the one named last changes fastest.
Arguments:
- resid: bfloat16 [8192, 2048], P('ep', 'grp'), may hold values from -6 to 6
- query: bfloat16 [8192, 2048], P('ep', 'grp'), may hold values from -6 to 6
- key_new: bfloat16 [8192, 2048], P('ep', 'grp'), may hold values from -6 to 6
- value_new: bfloat16 [8192, 2048], P('ep', 'grp'), may hold values from -6 to 6
- cache_kv: bfloat16 [2, 65536, 2048], P(None, 'ep', 'grp'), may hold values from -6 to 6
- cache_len: int32 [64], replicated, may hold values from 1 to 1024, 16384 in all
- w_out: bfloat16 [2048, 2048], P('grp'), may hold values from -0.125 to 0.125
- norm_gain: bfloat16 [2048], replicated, may hold values from 0.099609375 to 1.8984375
- w_router: bfloat16 [2048, 64], replicated, may hold values from -7 to 7
- routes: int32 [8192, 4], P('ep'), may hold values from 0 to 63, all different within a row; in each aligned block of 128 rows (0 to 127, 128 to 255, ...) at most 16 rows name the same one
- w_gate_up: bfloat16 [64, 2, 2048, 1408], P('ep', None, None, 'grp'), may hold values from -0.125 to 0.125
- w_down: bfloat16 [64, 1408, 2048], P('ep', 'grp'), may hold values from -0.15625 to 0.15625
Outputs:
- after_attention: bfloat16 [8192, 2048], P('ep', 'grp')
- expert_mix: bfloat16 [8192, 2048], P('ep', 'grp')
The draws below stay inside these ranges and needn't reach their ends.
Inputs may be any that keep to these rules, and one draw needn't show every extreme that they name: `routes`: in each aligned block of 128 rows (one request's tokens), no expert is named by more than 16 of the pairs, and in every draw some expert is named by exactly 16. Request r's cache fills the first cache_len[r] rows of its slab, rows r * 1024 onward of cache_kv; the rest of the slab is unused; the lengths sum to 16384 and the longest is exactly 1024.
All inputs are finite; a program needn't handle non-finite values.
Results may differ from the reference program's by a relative error of at most 0.013.
Values may be sent and summed in bfloat16 or wider, within the bound.
No kernel may reach another device: no remote copies, remote signals or barrier semaphores. Data moves between devices by JAX's collectives and lax.ppermute only.
A program may use at most 64 MiB of HBM per device.

```python
import math
import jax
import jax.numpy as jnp
import numpy as np
from jax import lax

D = 2048
HEADS = 16
HD = 128
FFE = 1408
TOP = 4
TOK_DEV = 128
CACHE_DEV = 1024
REQUESTS = 64
EXPERTS = 64
TOKENS = 8192
CACHE = 65536
CACHED = 16384
CAP = 16
SLICE = 176
N_GRP = 8
N_EP = 64


ROUTER_SPREAD = 0.5


def drawn_normal(key, salt, shape):
    return jnp.clip(jax.random.normal(jax.random.fold_in(key, salt), shape, jnp.float32), -6.0, 6.0)


def draw_query(key, part):
    values_drawn = drawn_normal(key, 1, (TOKENS, HEADS * HD))
    return values_drawn.astype(jnp.bfloat16)


def draw_key_new(key, part):
    values_drawn = drawn_normal(key, 2, (TOKENS, HEADS * HD))
    return values_drawn.astype(jnp.bfloat16)


def draw_resid(key, part):
    values_drawn = drawn_normal(key, 3, (TOKENS, D))
    return values_drawn.astype(jnp.bfloat16)


def draw_w_router(key, part):
    values_drawn = drawn_normal(key, 4, (D, EXPERTS)) * (ROUTER_SPREAD * float(D) ** (-0.5))
    return values_drawn.astype(jnp.bfloat16)


def shard_levels(rng, extent, cuts, low, top_value):
    loudness, own = 1.0, jax.random.fold_in(rng, 6)
    for axis_at, shards_of in cuts:
        heights = jnp.exp(jax.random.uniform(jax.random.fold_in(own, axis_at), (shards_of,), jnp.float32, low / len(cuts), top_value / len(cuts)))
        loudness = loudness * jnp.repeat(heights, extent[axis_at] // shards_of).reshape([-1 if axis == axis_at else 1 for axis in range(len(extent))])
    return loudness


def length_profile(amount, total, most, lean):
    portions = [(1 << 20) // math.isqrt(grade ** lean) + 1 for grade in range(2, amount + 1)]
    surplus, counts = total - most - (amount - 1), [1] * (amount - 1)
    while surplus > 0:
        free = [i for i in range(amount - 1) if counts[i] < most]
        mass, left = sum([portions[i] for i in free]), surplus
        for i in free:
            extra = min(most - counts[i], max(1, left * portions[i] // mass), surplus)
            counts[i] = counts[i] + extra
            surplus = surplus - extra
    return np.array([most] + counts)


def ragged_sizes(own_key, number_of, total, bound, lean):
    if number_of == 2:
        one = jax.random.randint(own_key, (), max(1, total - bound), min(bound, total - 1) + 1)
        return jnp.stack([one, total - one])
    sizes = jnp.asarray(length_profile(number_of, total, bound, lean), jnp.int32)
    couples = (number_of - 1) // 2
    source_of, taker = sizes[1:1 + 2 * couples:2], sizes[2:2 + 2 * couples:2]
    margin = jnp.minimum(source_of - 1, bound - taker)
    shifted = jax.random.randint(jax.random.fold_in(own_key, 1), (couples,), 0, 1 << 20) % (margin + 1)
    sizes = sizes.at[1:1 + 2 * couples:2].set(source_of - shifted).at[2:2 + 2 * couples:2].set(taker + shifted)
    return sizes[jax.random.permutation(jax.random.fold_in(own_key, 2), number_of)]


def assign_block(key, own, number, rows, amount, top, bound, lean):
    ranking = jax.random.permutation(key, amount)
    crowded, ordinary = portions_of(amount, rows * top, bound, lean, True), portions_of(amount, rows * top, bound, lean, False)
    places = jnp.arange(amount)

    def named(sizes, turn):
        used = int((sizes > 0).sum())
        fixed = max(1, used // 4)
        passed = fixed + (places - fixed + turn * (used - fixed)) % max(1, amount - fixed)
        return jnp.zeros((amount,), jnp.int32).at[ranking[jnp.where(places < fixed, places, passed)]].set(jnp.asarray(sizes, jnp.int32))

    sizes = jnp.where(number % 4 == 0, named(crowded, number // 4), named(ordinary, number - number // 4 - 1))
    mixed = jax.random.permutation(jax.random.fold_in(own, 3), amount)
    giver, taker = mixed[0:amount // 2 * 2:2], mixed[1:amount // 2 * 2:2]
    margin = jnp.minimum(sizes[giver] - 1, bound - sizes[taker]) // 2
    margin = jnp.where((giver == ranking[0]) | (taker == ranking[0]) | (sizes[taker] == 0), 0, jnp.maximum(margin, 0))
    passed = jax.random.randint(jax.random.fold_in(own, 4), (amount // 2,), 0, 1 << 20) % (margin + 1)
    sizes = sizes.at[giver].add(-passed).at[taker].add(passed)
    members = jnp.searchsorted(jnp.cumsum(sizes), jnp.arange(rows * top), side="right").astype(jnp.int32)
    table = members.reshape(top, rows).T
    table = table[jax.random.permutation(jax.random.fold_in(own, 1), rows)]
    turn = jax.random.randint(jax.random.fold_in(own, 2), (rows, 1), 0, top)
    return jnp.take_along_axis(table, (jnp.arange(top)[None, :] + turn) % top, axis=1)


def portions_of(amount, total, most, lean, full):
    loads = [(1 << 20) // math.isqrt(rank ** lean) + 1 for rank in range(1, amount + 1)]
    largest = most if full else min(most, max(-(-total // amount), total * loads[0] // sum(loads)))
    least = 1 if total - largest >= amount - 1 else 0
    holding, spare = [largest] + [least] * (amount - 1), total - largest - least * (amount - 1)
    while spare > 0:
        free = [i for i in range(1, amount) if holding[i] < largest] or [i for i in range(1, amount) if holding[i] < most]
        pool, left = sum([loads[i] for i in free]), spare
        for i in free:
            addition = min(most - holding[i], max(1, left * loads[i] // pool), spare)
            holding[i] = holding[i] + addition
            spare = spare - addition
    return np.array(holding)


def gaussian(stream_key, shape, spread, bound, cuts=(), kind=jnp.bfloat16):
    drawn = jax.random.normal(stream_key, shape, jnp.float32) * spread
    if len(cuts) > 0:
        drawn = shard_levels(stream_key, shape, cuts, -0.22, 0.18) * drawn
    return jnp.clip(drawn, min=-bound, max=bound).astype(kind)


def setup_inputs(seed: int = 0) -> dict:
    splits = jax.random.split(jax.random.key(seed), 13)
    resid = draw_resid(jax.random.fold_in(splits[12], 71), 0)
    query = draw_query(jax.random.fold_in(splits[12], 71), 0)
    key_new = draw_key_new(jax.random.fold_in(splits[12], 71), 0)
    value_new = gaussian(splits[3], (TOKENS, HEADS * HD), 1.0, 6.0, ((0, 64), (1, 8)))
    cache_kv = gaussian(splits[4], (2, CACHE, HEADS * HD), 1.0, 6.0, ((1, 64), (2, 8)))
    cache_len = ragged_sizes(splits[5], REQUESTS, CACHED, CACHE_DEV, 2).astype(jnp.int32)
    w_out = gaussian(splits[6], (HEADS * HD, D), (HEADS * HD) ** -0.5, 0.125, ((0, 8),))
    norm_gain = jnp.clip(1.0 + 0.18 * jax.random.normal(splits[7], (D,), jnp.float32), 0.099609375, 1.8984375).astype(jnp.bfloat16)
    w_router = draw_w_router(jax.random.fold_in(splits[12], 71), 0)
    routes_keys = jax.random.split(jax.random.fold_in(splits[9], 1), TOKENS // TOK_DEV)
    routes_turns = jax.random.permutation(jax.random.fold_in(splits[9], 3), TOKENS // TOK_DEV)
    routes = jax.vmap(lambda own, number: assign_block(jax.random.fold_in(splits[9], 2), own, number, TOK_DEV, EXPERTS, TOP, CAP, 2))(routes_keys, routes_turns).reshape((TOKENS, TOP))
    w_gate_up = gaussian(splits[10], (EXPERTS, 2, D, FFE), D ** -0.5, 0.125, ((0, 64), (3, 8)))
    w_down = gaussian(splits[11], (EXPERTS, FFE, D), FFE ** -0.5, 0.15625, ((0, 64), (1, 8)))
    return {"resid": resid, "query": query, "key_new": key_new, "value_new": value_new, "cache_kv": cache_kv, "cache_len": cache_len, "w_out": w_out, "norm_gain": norm_gain, "w_router": w_router, "routes": routes, "w_gate_up": w_gate_up, "w_down": w_down}


EPS = 1e-06
MASKED = -1e+30

def attend(queries, new_keys, new_values, cache_keys, cache_values, length):
    score_scale = float(HD) ** (-0.5)
    queries = queries.astype(jnp.float32)
    new_keys = new_keys.astype(jnp.float32)
    new_values = new_values.astype(jnp.float32)
    cache_keys = cache_keys.astype(jnp.float32)
    cache_values = cache_values.astype(jnp.float32)
    position = jnp.arange(TOK_DEV, dtype=jnp.int32)
    new_scores = jnp.einsum('qhd,khd->qhk', queries, new_keys) * score_scale
    causal = (position[:, None] >= position[None, :])[:, None, :]
    new_scores = jnp.where(causal, new_scores, MASKED)
    cache_position = jnp.arange(CACHE_DEV, dtype=jnp.int32)
    live_rows = cache_position < length
    old_scores = jnp.einsum('qhd,khd->qhk', queries, cache_keys) * score_scale
    old_scores = jnp.where(live_rows[None, None, :], old_scores, MASKED)
    row_max = jnp.maximum(lax.optimization_barrier(jnp.max(new_scores, axis=-1)), lax.optimization_barrier(jnp.max(old_scores, axis=-1)))
    new_probs = jnp.exp(new_scores - row_max[..., None])
    old_probs = jnp.exp(old_scores - row_max[..., None])
    denominator = lax.optimization_barrier(jnp.sum(new_probs, axis=-1)) + lax.optimization_barrier(jnp.sum(old_probs, axis=-1))
    new_rounded = lax.optimization_barrier(new_probs.astype(jnp.bfloat16)).astype(jnp.float32)
    old_rounded = lax.optimization_barrier(old_probs.astype(jnp.bfloat16)).astype(jnp.float32)
    weighted = jnp.einsum('qhk,khd->qhd', new_rounded, new_values) + jnp.einsum('qhk,khd->qhd', old_rounded, cache_values)
    return (weighted / denominator[..., None]).astype(jnp.bfloat16)

def reference(resid, query, key_new, value_new, cache_kv, cache_len, w_out, norm_gain, w_router, routes, w_gate_up, w_down):
    shaped = (REQUESTS, TOK_DEV, HEADS, HD)
    queries = query.reshape(shaped)
    new_keys = key_new.reshape(shaped)
    new_values = value_new.reshape(shaped)
    slabs = cache_kv.reshape(2, REQUESTS, CACHE_DEV, HEADS, HD)
    lengths = cache_len.astype(jnp.int32)

    def one_request(inputs):
        request_q, request_k, request_v, slab_keys, slab_values, length = inputs
        return attend(request_q, request_k, request_v, slab_keys, slab_values, length)
    attended = lax.map(one_request, (queries, new_keys, new_values, slabs[0], slabs[1], lengths))
    attended = attended.reshape(TOKENS, HEADS * HD)
    projected = jnp.dot(attended, w_out, preferred_element_type=jnp.float32)
    after_attention = (resid.astype(jnp.float32) + projected).astype(jnp.bfloat16)
    after_wide = after_attention.astype(jnp.float32)
    inverse = lax.rsqrt(lax.optimization_barrier(jnp.mean(after_wide * after_wide, axis=1)) + EPS)
    normed = (after_wide * inverse[:, None] * norm_gain.astype(jnp.float32)[None, :]).astype(jnp.bfloat16)
    logits = jnp.dot(normed, w_router, preferred_element_type=jnp.float32)
    chosen = jnp.take_along_axis(logits, routes.astype(jnp.int32), axis=1)
    route_weight = jax.nn.softmax(chosen, axis=-1).astype(jnp.bfloat16)
    pairs = routes.astype(jnp.int32).reshape(N_EP, TOK_DEV * TOP)
    route_hits = (pairs[:, :, None] == jnp.arange(EXPERTS, dtype=jnp.int32)[None, None, :]).astype(jnp.int32)
    earlier = jnp.cumsum(route_hits, axis=1) - route_hits
    slot_index = lax.optimization_barrier(jnp.sum(earlier * route_hits, axis=2))
    block_index = jnp.arange(N_EP, dtype=jnp.int32)[:, None]
    row_id = (pairs * (N_EP * CAP) + block_index * CAP + slot_index).reshape(-1).astype(jnp.int32)
    sources = jnp.repeat(normed, TOP, axis=0)
    expert_input = jnp.zeros((EXPERTS * N_EP * CAP, D), jnp.bfloat16).at[row_id].set(sources)
    expert_input = expert_input.reshape(EXPERTS, N_EP * CAP, D)

    def one_expert(inputs):
        rows_in, gate_up, down_rows = inputs
        gate_value = jnp.dot(rows_in, gate_up[0], preferred_element_type=jnp.float32)
        up_value = jnp.dot(rows_in, gate_up[1], preferred_element_type=jnp.float32)
        hidden = (jax.nn.silu(gate_value) * up_value).astype(jnp.bfloat16)
        summed = jnp.zeros((rows_in.shape[0], D), jnp.float32)
        for group_number in range(N_GRP):
            partial_value = jnp.dot(hidden[:, group_number * SLICE:(group_number + 1) * SLICE], down_rows[group_number * SLICE:(group_number + 1) * SLICE], preferred_element_type=jnp.float32).astype(jnp.bfloat16)
            summed = summed + lax.optimization_barrier(partial_value).astype(jnp.float32)
        return summed
    expert_out = lax.map(one_expert, (expert_input, w_gate_up, w_down)).reshape(EXPERTS * N_EP * CAP, D)
    picked = expert_out[row_id].reshape(TOKENS, TOP, D)
    expert_mix = lax.optimization_barrier(jnp.sum(picked * route_weight.astype(jnp.float32)[:, :, None], axis=1))
    return (after_attention, expert_mix.astype(jnp.bfloat16))
```

```python
import jax
import jax.numpy as jnp
from jax import lax
from jax.sharding import PartitionSpec as P

D = 2048
HD = 128
TOP = 4


EPS = 1e-06
MASKED = -1e30


def body(
    resid,
    query,
    key_new,
    value_new,
    cache_kv,
    cache_len,
    w_out,
    norm_gain,
    w_router,
    routes,
    w_gate_up,
    w_down,
):
    tokens_here = query.shape[0]
    heads_here = query.shape[1] // HD
    experts_all = w_router.shape[1]
    column_width = resid.shape[1]
    group_index = lax.axis_index("grp")
    request = lax.axis_index("ep")
    capacity = max(2, 8 * tokens_here // lax.axis_size("ep"))
    score_scale = float(HD) ** (-0.5)
    column_start = group_index * column_width
    queries = query.reshape(tokens_here, heads_here, HD)
    new_keys = key_new.reshape(tokens_here, heads_here, HD)
    new_values = value_new.reshape(tokens_here, heads_here, HD)
    cache_rows = cache_kv.shape[1]
    cache_keys = cache_kv[0].reshape(cache_rows, heads_here, HD)
    cache_values = cache_kv[1].reshape(cache_rows, heads_here, HD)
    own_length = lax.dynamic_index_in_dim(cache_len, request, 0, keepdims=False)
    position = jnp.arange(tokens_here, dtype=jnp.int32)
    causal = (position[:, None] >= position[None, :])[:, None, :]
    new_scores = (
        jnp.einsum("qhd,khd->qhk", queries, new_keys, preferred_element_type=jnp.float32)
        * score_scale
    )
    new_scores = jnp.where(causal, new_scores, MASKED)
    live_rows = (jnp.arange(cache_rows, dtype=jnp.int32) < own_length)[None, None, :]
    old_scores = (
        jnp.einsum("qhd,khd->qhk", queries, cache_keys, preferred_element_type=jnp.float32)
        * score_scale
    )
    old_scores = jnp.where(live_rows, old_scores, MASKED)
    row_max = jnp.maximum(jnp.max(new_scores, axis=-1), jnp.max(old_scores, axis=-1))
    new_probs = jnp.exp(new_scores - row_max[..., None])
    old_probs = jnp.exp(old_scores - row_max[..., None])
    denominator = jnp.sum(new_probs, axis=-1) + jnp.sum(old_probs, axis=-1)
    weighted = jnp.einsum(
        "qhk,khd->qhd",
        new_probs.astype(jnp.bfloat16),
        new_values,
        preferred_element_type=jnp.float32,
    )
    weighted = weighted + jnp.einsum(
        "qhk,khd->qhd",
        old_probs.astype(jnp.bfloat16),
        cache_values,
        preferred_element_type=jnp.float32,
    )
    attended = (
        (weighted / denominator[..., None])
        .astype(jnp.bfloat16)
        .reshape(tokens_here, heads_here * HD)
    )
    projected = jnp.dot(attended, w_out, preferred_element_type=jnp.float32)
    attn_share = lax.psum_scatter(projected, "grp", scatter_dimension=1, tiled=True)
    after_cols = (resid.astype(jnp.float32) + attn_share).astype(jnp.bfloat16)
    after_full = lax.all_gather(after_cols, "grp", axis=1, tiled=True)
    after_wide = after_full.astype(jnp.float32)
    squares = jnp.sum(after_wide * after_wide, axis=1)
    inverse = lax.rsqrt(squares / D + EPS)
    normed_full = (
        after_wide * inverse[:, None] * norm_gain.astype(jnp.float32)[None, :]
    ).astype(jnp.bfloat16)
    normed_cols = lax.dynamic_slice_in_dim(normed_full, column_start, column_width, 1)
    logits = jnp.dot(normed_full, w_router, preferred_element_type=jnp.float32)
    route_hits = routes[:, :, None] == jnp.arange(experts_all, dtype=jnp.int32)[None, None, :]
    chosen = jnp.sum(jnp.where(route_hits, logits[:, None, :], 0.0), axis=-1)
    route_weight = jax.nn.softmax(chosen, axis=-1).astype(jnp.bfloat16)
    flat_hits = route_hits.reshape(tokens_here * TOP, experts_all).astype(jnp.int32)
    earlier = jnp.cumsum(flat_hits, axis=0) - flat_hits
    slot_index = jnp.sum(earlier * flat_hits, axis=1)
    slot_row = (routes.reshape(-1) * capacity + slot_index).reshape(tokens_here, TOP)
    slot_ids = jnp.arange(experts_all * capacity, dtype=jnp.int32)
    matches = slot_row[:, :, None] == slot_ids[None, None, :]
    selection = jnp.any(matches, axis=1).astype(jnp.bfloat16)
    combine = jnp.sum(
        jnp.where(matches, route_weight[:, :, None].astype(jnp.float32), 0.0), axis=1
    )
    outgoing = jnp.einsum(
        "tj,td->jd", selection, normed_cols, preferred_element_type=jnp.float32
    ).astype(jnp.bfloat16)
    outgoing = outgoing.reshape(experts_all, capacity, column_width)
    arrived = lax.all_to_all(outgoing, "ep", split_axis=0, concat_axis=0, tiled=True)
    arrived = arrived.reshape(experts_all * capacity, column_width)
    groups = lax.axis_size("grp")
    gathered = lax.all_gather(arrived, "grp", axis=0, tiled=False)
    slice_width = w_gate_up.shape[-1]
    gate_up = w_gate_up[0].reshape(2, groups, column_width, slice_width)
    gate_value = jnp.einsum(
        "gnc,gch->nh", gathered, gate_up[0], preferred_element_type=jnp.float32
    )
    up_value = jnp.einsum("gnc,gch->nh", gathered, gate_up[1], preferred_element_type=jnp.float32)
    hidden = (jax.nn.silu(gate_value) * up_value).astype(jnp.bfloat16)
    down = w_down[0].reshape(slice_width, groups, column_width)
    slice_out = jnp.einsum(
        "nh,hgc->gnc", hidden, down, preferred_element_type=jnp.float32
    ).astype(jnp.bfloat16)
    slices_here = lax.all_to_all(slice_out, "grp", split_axis=0, concat_axis=0, tiled=True)
    expert_out = jnp.sum(slices_here.astype(jnp.float32), axis=0)
    expert_out = expert_out.reshape(experts_all, capacity, column_width)
    returned = lax.all_to_all(expert_out, "ep", split_axis=0, concat_axis=0, tiled=True)
    mixed_cols = jnp.dot(
        combine,
        returned.reshape(experts_all * capacity, column_width),
        precision=lax.Precision.HIGHEST,
        preferred_element_type=jnp.float32,
    )
    return (after_cols, mixed_cols.astype(jnp.bfloat16))


def solution(mesh):
    return jax.shard_map(
        body,
        mesh=mesh,
        in_specs=(
            P("ep", "grp"),
            P("ep", "grp"),
            P("ep", "grp"),
            P("ep", "grp"),
            P(None, "ep", "grp"),
            P(),
            P("grp", None),
            P(),
            P(),
            P("ep", None),
            P("ep", None, None, "grp"),
            P("ep", "grp", None),
        ),
        out_specs=(P("ep", "grp"), P("ep", "grp")),
        check_vma=False,
    )
```

```python
import jax
import jax.numpy as jnp
from jax import lax
from jax.sharding import PartitionSpec as P

D = 2048
HD = 128
TOP = 4


EPS = 1e-06
MASKED = -1e30


def body(
    resid,
    query,
    key_new,
    value_new,
    cache_kv,
    cache_len,
    w_out,
    norm_gain,
    w_router,
    routes,
    w_gate_up,
    w_down,
):
    tokens_here = query.shape[0]
    heads_here = query.shape[1] // HD
    experts_all = w_router.shape[1]
    column_width = resid.shape[1]
    group_index = lax.axis_index("grp")
    request = lax.axis_index("ep")
    capacity = max(2, 8 * tokens_here // lax.axis_size("ep"))
    score_scale = float(HD) ** (-0.5)
    column_start = group_index * column_width
    queries = query.reshape(tokens_here, heads_here, HD)
    new_keys = key_new.reshape(tokens_here, heads_here, HD)
    new_values = value_new.reshape(tokens_here, heads_here, HD)
    cache_rows = cache_kv.shape[1]
    cache_keys = cache_kv[0].reshape(cache_rows, heads_here, HD)
    cache_values = cache_kv[1].reshape(cache_rows, heads_here, HD)
    own_length = lax.dynamic_index_in_dim(cache_len, request, 0, keepdims=False)
    position = jnp.arange(tokens_here, dtype=jnp.int32)
    causal = (position[:, None] >= position[None, :])[:, None, :]
    new_scores = (
        jnp.einsum("qhd,khd->qhk", queries, new_keys, preferred_element_type=jnp.float32)
        * score_scale
    )
    new_scores = jnp.where(causal, new_scores, MASKED)
    live_rows = (jnp.arange(cache_rows, dtype=jnp.int32) < own_length)[None, None, :]
    old_scores = (
        jnp.einsum("qhd,khd->qhk", queries, cache_keys, preferred_element_type=jnp.float32)
        * score_scale
    )
    old_scores = jnp.where(live_rows, old_scores, MASKED)
    row_max = jnp.maximum(jnp.max(new_scores, axis=-1), jnp.max(old_scores, axis=-1))
    new_probs = jnp.exp(new_scores - row_max[..., None])
    old_probs = jnp.exp(old_scores - row_max[..., None])
    denominator = jnp.sum(new_probs, axis=-1) + jnp.sum(old_probs, axis=-1)
    weighted = jnp.einsum(
        "qhk,khd->qhd",
        new_probs.astype(jnp.bfloat16),
        new_values,
        preferred_element_type=jnp.float32,
    )
    weighted = weighted + jnp.einsum(
        "qhk,khd->qhd",
        old_probs.astype(jnp.bfloat16),
        cache_values,
        preferred_element_type=jnp.float32,
    )
    attended = (
        (weighted / denominator[..., None])
        .astype(jnp.bfloat16)
        .reshape(tokens_here, heads_here * HD)
    )
    projected = jnp.dot(attended, w_out, preferred_element_type=jnp.float32)
    attn_share = lax.psum_scatter(
        projected.astype(jnp.bfloat16), "grp", scatter_dimension=1, tiled=True
    )
    after_cols = (resid.astype(jnp.float32) + attn_share.astype(jnp.float32)).astype(jnp.bfloat16)
    after_full = lax.all_gather(after_cols, "grp", axis=1, tiled=True)
    after_wide = after_full.astype(jnp.float32)
    squares = jnp.sum(after_wide * after_wide, axis=1)
    inverse = lax.rsqrt(squares / D + EPS)
    normed_full = (
        after_wide * inverse[:, None] * norm_gain.astype(jnp.float32)[None, :]
    ).astype(jnp.bfloat16)
    normed_cols = lax.dynamic_slice_in_dim(normed_full, column_start, column_width, 1)
    logits = jnp.dot(normed_full, w_router, preferred_element_type=jnp.float32)
    route_hits = routes[:, :, None] == jnp.arange(experts_all, dtype=jnp.int32)[None, None, :]
    chosen = jnp.sum(jnp.where(route_hits, logits[:, None, :], 0.0), axis=-1)
    route_weight = jax.nn.softmax(chosen, axis=-1).astype(jnp.bfloat16)
    flat_hits = route_hits.reshape(tokens_here * TOP, experts_all).astype(jnp.int32)
    earlier = jnp.cumsum(flat_hits, axis=0) - flat_hits
    slot_index = jnp.sum(earlier * flat_hits, axis=1)
    slot_row = (routes.reshape(-1) * capacity + slot_index).reshape(tokens_here, TOP)
    slot_ids = jnp.arange(experts_all * capacity, dtype=jnp.int32)
    matches = slot_row[:, :, None] == slot_ids[None, None, :]
    selection = jnp.any(matches, axis=1).astype(jnp.bfloat16)
    combine = jnp.sum(
        jnp.where(matches, route_weight[:, :, None].astype(jnp.float32), 0.0), axis=1
    )
    outgoing = jnp.einsum(
        "tj,td->jd", selection, normed_cols, preferred_element_type=jnp.float32
    ).astype(jnp.bfloat16)
    outgoing = outgoing.reshape(experts_all, capacity, column_width)
    arrived = lax.all_to_all(outgoing, "ep", split_axis=0, concat_axis=0, tiled=True)
    arrived = arrived.reshape(experts_all * capacity, column_width)
    groups = lax.axis_size("grp")
    gathered = lax.all_gather(arrived, "grp", axis=0, tiled=False)
    slice_width = w_gate_up.shape[-1]
    gate_up = w_gate_up[0].reshape(2, groups, column_width, slice_width)
    gate_value = jnp.einsum(
        "gnc,gch->nh", gathered, gate_up[0], preferred_element_type=jnp.float32
    )
    up_value = jnp.einsum("gnc,gch->nh", gathered, gate_up[1], preferred_element_type=jnp.float32)
    hidden = (jax.nn.silu(gate_value) * up_value).astype(jnp.bfloat16)
    down = w_down[0].reshape(slice_width, groups, column_width)
    slice_out = jnp.einsum(
        "nh,hgc->gnc", hidden, down, preferred_element_type=jnp.float32
    ).astype(jnp.bfloat16)
    expert_out = lax.psum_scatter(slice_out, "grp", scatter_dimension=0, tiled=True)
    expert_out = expert_out.reshape(experts_all, capacity, column_width)
    returned = lax.all_to_all(expert_out, "ep", split_axis=0, concat_axis=0, tiled=True)
    mixed_cols = jnp.dot(
        combine,
        returned.reshape(experts_all * capacity, column_width),
        precision=lax.Precision.HIGHEST,
        preferred_element_type=jnp.float32,
    )
    return (after_cols, mixed_cols.astype(jnp.bfloat16))


def solution(mesh):
    return jax.shard_map(
        body,
        mesh=mesh,
        in_specs=(
            P("ep", "grp"),
            P("ep", "grp"),
            P("ep", "grp"),
            P("ep", "grp"),
            P(None, "ep", "grp"),
            P(),
            P("grp", None),
            P(),
            P(),
            P("ep", None),
            P("ep", None, None, "grp"),
            P("ep", "grp", None),
        ),
        out_specs=(P("ep", "grp"), P("ep", "grp")),
        check_vma=False,
    )
```

```python
import jax
import jax.numpy as jnp
from jax import lax
from jax.sharding import PartitionSpec as P

D = 2048
HD = 128
TOP = 4


EPS = 1e-06
MASKED = -1e30


def body(
    resid,
    query,
    key_new,
    value_new,
    cache_kv,
    cache_len,
    w_out,
    norm_gain,
    w_router,
    routes,
    w_gate_up,
    w_down,
):
    tokens_here = query.shape[0]
    heads_here = query.shape[1] // HD
    experts_all = w_router.shape[1]
    column_width = resid.shape[1]
    group_index = lax.axis_index("grp")
    request = lax.axis_index("ep")
    capacity = max(2, 8 * tokens_here // lax.axis_size("ep"))
    score_scale = float(HD) ** (-0.5)
    column_start = group_index * column_width
    queries = query.reshape(tokens_here, heads_here, HD)
    new_keys = key_new.reshape(tokens_here, heads_here, HD)
    new_values = value_new.reshape(tokens_here, heads_here, HD)
    cache_rows = cache_kv.shape[1]
    cache_keys = cache_kv[0].reshape(cache_rows, heads_here, HD)
    cache_values = cache_kv[1].reshape(cache_rows, heads_here, HD)
    own_length = lax.dynamic_index_in_dim(cache_len, request, 0, keepdims=False)
    position = jnp.arange(tokens_here, dtype=jnp.int32)
    causal = (position[:, None] >= position[None, :])[:, None, :]
    new_scores = (
        jnp.einsum("qhd,khd->qhk", queries, new_keys, preferred_element_type=jnp.float32)
        * score_scale
    )
    new_scores = jnp.where(causal, new_scores, MASKED)
    live_rows = (jnp.arange(cache_rows, dtype=jnp.int32) < own_length)[None, None, :]
    old_scores = (
        jnp.einsum("qhd,khd->qhk", queries, cache_keys, preferred_element_type=jnp.float32)
        * score_scale
    )
    old_scores = jnp.where(live_rows, old_scores, MASKED)
    row_max = jnp.maximum(jnp.max(new_scores, axis=-1), jnp.max(old_scores, axis=-1))
    new_probs = jnp.exp(new_scores - row_max[..., None])
    old_probs = jnp.exp(old_scores - row_max[..., None])
    denominator = jnp.sum(new_probs, axis=-1) + jnp.sum(old_probs, axis=-1)
    weighted = jnp.einsum(
        "qhk,khd->qhd",
        new_probs.astype(jnp.bfloat16),
        new_values,
        preferred_element_type=jnp.float32,
    )
    weighted = weighted + jnp.einsum(
        "qhk,khd->qhd",
        old_probs.astype(jnp.bfloat16),
        cache_values,
        preferred_element_type=jnp.float32,
    )
    attended = (
        (weighted / denominator[..., None])
        .astype(jnp.bfloat16)
        .reshape(tokens_here, heads_here * HD)
    )
    projected = jnp.dot(attended, w_out, preferred_element_type=jnp.float32)
    projected_full = lax.psum(projected, "grp")
    resid_full = lax.all_gather(resid, "grp", axis=1, tiled=True)
    after_full = (resid_full.astype(jnp.float32) + projected_full).astype(jnp.bfloat16)
    after_cols = lax.dynamic_slice_in_dim(after_full, column_start, column_width, 1)
    after_wide = after_full.astype(jnp.float32)
    squares = jnp.sum(after_wide * after_wide, axis=1)
    inverse = lax.rsqrt(squares / D + EPS)
    normed_full = (
        after_wide * inverse[:, None] * norm_gain.astype(jnp.float32)[None, :]
    ).astype(jnp.bfloat16)
    normed_cols = lax.dynamic_slice_in_dim(normed_full, column_start, column_width, 1)
    logits = jnp.dot(normed_full, w_router, preferred_element_type=jnp.float32)
    route_hits = routes[:, :, None] == jnp.arange(experts_all, dtype=jnp.int32)[None, None, :]
    chosen = jnp.sum(jnp.where(route_hits, logits[:, None, :], 0.0), axis=-1)
    route_weight = jax.nn.softmax(chosen, axis=-1).astype(jnp.bfloat16)
    flat_hits = route_hits.reshape(tokens_here * TOP, experts_all).astype(jnp.int32)
    earlier = jnp.cumsum(flat_hits, axis=0) - flat_hits
    slot_index = jnp.sum(earlier * flat_hits, axis=1)
    slot_row = (routes.reshape(-1) * capacity + slot_index).reshape(tokens_here, TOP)
    slot_ids = jnp.arange(experts_all * capacity, dtype=jnp.int32)
    matches = slot_row[:, :, None] == slot_ids[None, None, :]
    selection = jnp.any(matches, axis=1).astype(jnp.bfloat16)
    combine = jnp.sum(
        jnp.where(matches, route_weight[:, :, None].astype(jnp.float32), 0.0), axis=1
    )
    outgoing = jnp.einsum(
        "tj,td->jd", selection, normed_cols, preferred_element_type=jnp.float32
    ).astype(jnp.bfloat16)
    outgoing = outgoing.reshape(experts_all, capacity, column_width)
    arrived = lax.all_to_all(outgoing, "ep", split_axis=0, concat_axis=0, tiled=True)
    arrived = arrived.reshape(experts_all * capacity, column_width)
    groups = lax.axis_size("grp")
    gathered = lax.all_gather(arrived, "grp", axis=0, tiled=False)
    slice_width = w_gate_up.shape[-1]
    gate_up = w_gate_up[0].reshape(2, groups, column_width, slice_width)
    gate_value = jnp.einsum(
        "gnc,gch->nh", gathered, gate_up[0], preferred_element_type=jnp.float32
    )
    up_value = jnp.einsum("gnc,gch->nh", gathered, gate_up[1], preferred_element_type=jnp.float32)
    hidden = (jax.nn.silu(gate_value) * up_value).astype(jnp.bfloat16)
    down = w_down[0].reshape(slice_width, groups, column_width)
    slice_out = jnp.einsum(
        "nh,hgc->gnc", hidden, down, preferred_element_type=jnp.float32
    ).astype(jnp.bfloat16)
    expert_out = lax.psum_scatter(slice_out, "grp", scatter_dimension=0, tiled=True)
    expert_out = expert_out.reshape(experts_all, capacity, column_width)
    returned = lax.all_to_all(expert_out, "ep", split_axis=0, concat_axis=0, tiled=True)
    mixed_cols = jnp.dot(
        combine,
        returned.reshape(experts_all * capacity, column_width),
        precision=lax.Precision.HIGHEST,
        preferred_element_type=jnp.float32,
    )
    return (after_cols, mixed_cols.astype(jnp.bfloat16))


def solution(mesh):
    return jax.shard_map(
        body,
        mesh=mesh,
        in_specs=(
            P("ep", "grp"),
            P("ep", "grp"),
            P("ep", "grp"),
            P("ep", "grp"),
            P(None, "ep", "grp"),
            P(),
            P("grp", None),
            P(),
            P(),
            P("ep", None),
            P("ep", None, None, "grp"),
            P("ep", "grp", None),
        ),
        out_specs=(P("ep", "grp"), P("ep", "grp")),
        check_vma=False,
    )
```

```python
import jax
import jax.numpy as jnp
from jax import lax
from jax.experimental import pallas as pl
from jax.sharding import PartitionSpec as P

D = 2048
HD = 128
TOP = 4


EPS = 1e-06
MASKED = -1e30


def ffn_kernel(x_ref, gu_ref, down_ref, out_ref):
    groups, rows, width = x_ref.shape
    gate = jnp.zeros((rows, gu_ref.shape[-1]), jnp.float32)
    up = jnp.zeros((rows, gu_ref.shape[-1]), jnp.float32)
    for g in range(groups):
        x = x_ref[g]
        gate = gate + jnp.dot(
            x, gu_ref[0, g * width:(g + 1) * width, :], preferred_element_type=jnp.float32
        )
        up = up + jnp.dot(
            x, gu_ref[1, g * width:(g + 1) * width, :], preferred_element_type=jnp.float32
        )
    hidden = (jax.nn.silu(gate) * up).astype(jnp.bfloat16)
    for g in range(groups):
        out_ref[g] = jnp.dot(
            hidden, down_ref[:, g * width:(g + 1) * width], preferred_element_type=jnp.float32
        ).astype(out_ref.dtype)


def expert_ffn(gathered, gate_up, down, row_tile=256):
    groups, rows, width = gathered.shape
    return pl.pallas_call(
        ffn_kernel,
        grid=(rows // row_tile,),
        in_specs=[
            pl.BlockSpec((groups, row_tile, width), lambda i: (0, i, 0)),
            pl.BlockSpec(gate_up.shape, lambda i: (0, 0, 0)),
            pl.BlockSpec(down.shape, lambda i: (0, 0)),
        ],
        out_specs=pl.BlockSpec((groups, row_tile, width), lambda i: (0, i, 0)),
        out_shape=jax.ShapeDtypeStruct(gathered.shape, jnp.bfloat16),
    )(gathered, gate_up, down)


def body(
    resid,
    query,
    key_new,
    value_new,
    cache_kv,
    cache_len,
    w_out,
    norm_gain,
    w_router,
    routes,
    w_gate_up,
    w_down,
):
    tokens_here = query.shape[0]
    heads_here = query.shape[1] // HD
    experts_all = w_router.shape[1]
    column_width = resid.shape[1]
    group_index = lax.axis_index("grp")
    request = lax.axis_index("ep")
    capacity = max(2, 8 * tokens_here // lax.axis_size("ep"))
    score_scale = float(HD) ** (-0.5)
    column_start = group_index * column_width
    queries = query.reshape(tokens_here, heads_here, HD)
    new_keys = key_new.reshape(tokens_here, heads_here, HD)
    new_values = value_new.reshape(tokens_here, heads_here, HD)
    cache_rows = cache_kv.shape[1]
    cache_keys = cache_kv[0].reshape(cache_rows, heads_here, HD)
    cache_values = cache_kv[1].reshape(cache_rows, heads_here, HD)
    own_length = lax.dynamic_index_in_dim(cache_len, request, 0, keepdims=False)
    position = jnp.arange(tokens_here, dtype=jnp.int32)
    causal = (position[:, None] >= position[None, :])[:, None, :]
    new_scores = (
        jnp.einsum("qhd,khd->qhk", queries, new_keys, preferred_element_type=jnp.float32)
        * score_scale
    )
    new_scores = jnp.where(causal, new_scores, MASKED)
    live_rows = (jnp.arange(cache_rows, dtype=jnp.int32) < own_length)[None, None, :]
    old_scores = (
        jnp.einsum("qhd,khd->qhk", queries, cache_keys, preferred_element_type=jnp.float32)
        * score_scale
    )
    old_scores = jnp.where(live_rows, old_scores, MASKED)
    row_max = jnp.maximum(jnp.max(new_scores, axis=-1), jnp.max(old_scores, axis=-1))
    new_probs = jnp.exp(new_scores - row_max[..., None])
    old_probs = jnp.exp(old_scores - row_max[..., None])
    denominator = jnp.sum(new_probs, axis=-1) + jnp.sum(old_probs, axis=-1)
    weighted = jnp.einsum(
        "qhk,khd->qhd",
        new_probs.astype(jnp.bfloat16),
        new_values,
        preferred_element_type=jnp.float32,
    )
    weighted = weighted + jnp.einsum(
        "qhk,khd->qhd",
        old_probs.astype(jnp.bfloat16),
        cache_values,
        preferred_element_type=jnp.float32,
    )
    attended = (
        (weighted / denominator[..., None])
        .astype(jnp.bfloat16)
        .reshape(tokens_here, heads_here * HD)
    )
    projected = jnp.dot(attended, w_out, preferred_element_type=jnp.float32)
    attn_share = lax.psum_scatter(projected, "grp", scatter_dimension=1, tiled=True)
    after_cols = (resid.astype(jnp.float32) + attn_share).astype(jnp.bfloat16)
    after_full = lax.all_gather(after_cols, "grp", axis=1, tiled=True)
    after_wide = after_full.astype(jnp.float32)
    squares = jnp.sum(after_wide * after_wide, axis=1)
    inverse = lax.rsqrt(squares / D + EPS)
    normed_full = (
        after_wide * inverse[:, None] * norm_gain.astype(jnp.float32)[None, :]
    ).astype(jnp.bfloat16)
    normed_cols = lax.dynamic_slice_in_dim(normed_full, column_start, column_width, 1)
    logits = jnp.dot(normed_full, w_router, preferred_element_type=jnp.float32)
    route_hits = routes[:, :, None] == jnp.arange(experts_all, dtype=jnp.int32)[None, None, :]
    chosen = jnp.sum(jnp.where(route_hits, logits[:, None, :], 0.0), axis=-1)
    route_weight = jax.nn.softmax(chosen, axis=-1).astype(jnp.bfloat16)
    flat_hits = route_hits.reshape(tokens_here * TOP, experts_all).astype(jnp.int32)
    earlier = jnp.cumsum(flat_hits, axis=0) - flat_hits
    slot_index = jnp.sum(earlier * flat_hits, axis=1)
    slot_row = (routes.reshape(-1) * capacity + slot_index).reshape(tokens_here, TOP)
    slot_ids = jnp.arange(experts_all * capacity, dtype=jnp.int32)
    matches = slot_row[:, :, None] == slot_ids[None, None, :]
    selection = jnp.any(matches, axis=1).astype(jnp.bfloat16)
    combine = jnp.sum(
        jnp.where(matches, route_weight[:, :, None].astype(jnp.float32), 0.0), axis=1
    )
    outgoing = jnp.einsum(
        "tj,td->jd", selection, normed_cols, preferred_element_type=jnp.float32
    ).astype(jnp.bfloat16)
    outgoing = outgoing.reshape(experts_all, capacity, column_width)
    arrived = lax.all_to_all(outgoing, "ep", split_axis=0, concat_axis=0, tiled=True)
    arrived = arrived.reshape(experts_all * capacity, column_width)
    groups = lax.axis_size("grp")
    gathered = lax.all_gather(arrived, "grp", axis=0, tiled=False)
    slice_out = expert_ffn(gathered, w_gate_up[0], w_down[0])
    expert_out = lax.psum_scatter(slice_out, "grp", scatter_dimension=0, tiled=True)
    expert_out = expert_out.reshape(experts_all, capacity, column_width)
    returned = lax.all_to_all(expert_out, "ep", split_axis=0, concat_axis=0, tiled=True)
    mixed_cols = jnp.dot(
        combine,
        returned.reshape(experts_all * capacity, column_width),
        precision=lax.Precision.HIGHEST,
        preferred_element_type=jnp.float32,
    )
    return (after_cols, mixed_cols.astype(jnp.bfloat16))


def solution(mesh):
    return jax.shard_map(
        body,
        mesh=mesh,
        in_specs=(
            P("ep", "grp"),
            P("ep", "grp"),
            P("ep", "grp"),
            P("ep", "grp"),
            P(None, "ep", "grp"),
            P(),
            P("grp", None),
            P(),
            P(),
            P("ep", None),
            P("ep", None, None, "grp"),
            P("ep", "grp", None),
        ),
        out_specs=(P("ep", "grp"), P("ep", "grp")),
        check_vma=False,
    )
```

```python
import math

import jax
import jax.numpy as jnp
from jax import lax
from jax.experimental import pallas as pl
from jax.sharding import Mesh
from jax.sharding import PartitionSpec as P

D = 2048
HD = 128
TOP = 4


EPS = 1e-06
MASKED = -1e30


def ffn_kernel(x_ref, gu_ref, down_ref, out_ref):
    groups, rows, width = x_ref.shape
    gate = jnp.zeros((rows, gu_ref.shape[-1]), jnp.float32)
    up = jnp.zeros((rows, gu_ref.shape[-1]), jnp.float32)
    for g in range(groups):
        x = x_ref[g]
        gate = gate + jnp.dot(
            x, gu_ref[0, g * width:(g + 1) * width, :], preferred_element_type=jnp.float32
        )
        up = up + jnp.dot(
            x, gu_ref[1, g * width:(g + 1) * width, :], preferred_element_type=jnp.float32
        )
    hidden = (jax.nn.silu(gate) * up).astype(jnp.bfloat16)
    for g in range(groups):
        out_ref[g] = jnp.dot(
            hidden, down_ref[:, g * width:(g + 1) * width], preferred_element_type=jnp.float32
        ).astype(out_ref.dtype)


def expert_ffn(gathered, gate_up, down, row_tile=256):
    groups, rows, width = gathered.shape
    return pl.pallas_call(
        ffn_kernel,
        grid=(rows // row_tile,),
        in_specs=[
            pl.BlockSpec((groups, row_tile, width), lambda i: (0, i, 0)),
            pl.BlockSpec(gate_up.shape, lambda i: (0, 0, 0)),
            pl.BlockSpec(down.shape, lambda i: (0, 0)),
        ],
        out_specs=pl.BlockSpec((groups, row_tile, width), lambda i: (0, i, 0)),
        out_shape=jax.ShapeDtypeStruct(gathered.shape, jnp.bfloat16),
    )(gathered, gate_up, down)


def body(
    resid,
    query,
    key_new,
    value_new,
    cache_kv,
    cache_len,
    w_out,
    norm_gain,
    w_router,
    routes,
    w_gate_up,
    w_down,
):
    tokens_here = query.shape[0]
    heads_here = query.shape[1] // HD
    experts_all = w_router.shape[1]
    column_width = resid.shape[1]
    group_index = lax.axis_index("grp")
    request = lax.axis_index("ez") * lax.axis_size("ey") + lax.axis_index("ey")
    ep_size = lax.axis_size("ez") * lax.axis_size("ey")
    capacity = max(2, 8 * tokens_here // ep_size)
    score_scale = float(HD) ** (-0.5)
    column_start = group_index * column_width
    queries = query.reshape(tokens_here, heads_here, HD)
    new_keys = key_new.reshape(tokens_here, heads_here, HD)
    new_values = value_new.reshape(tokens_here, heads_here, HD)
    cache_rows = cache_kv.shape[1]
    cache_keys = cache_kv[0].reshape(cache_rows, heads_here, HD)
    cache_values = cache_kv[1].reshape(cache_rows, heads_here, HD)
    own_length = lax.dynamic_index_in_dim(cache_len, request, 0, keepdims=False)
    position = jnp.arange(tokens_here, dtype=jnp.int32)
    causal = (position[:, None] >= position[None, :])[:, None, :]
    new_scores = (
        jnp.einsum("qhd,khd->qhk", queries, new_keys, preferred_element_type=jnp.float32)
        * score_scale
    )
    new_scores = jnp.where(causal, new_scores, MASKED)
    live_rows = (jnp.arange(cache_rows, dtype=jnp.int32) < own_length)[None, None, :]
    old_scores = (
        jnp.einsum("qhd,khd->qhk", queries, cache_keys, preferred_element_type=jnp.float32)
        * score_scale
    )
    old_scores = jnp.where(live_rows, old_scores, MASKED)
    row_max = jnp.maximum(jnp.max(new_scores, axis=-1), jnp.max(old_scores, axis=-1))
    new_probs = jnp.exp(new_scores - row_max[..., None])
    old_probs = jnp.exp(old_scores - row_max[..., None])
    denominator = jnp.sum(new_probs, axis=-1) + jnp.sum(old_probs, axis=-1)
    weighted = jnp.einsum(
        "qhk,khd->qhd",
        new_probs.astype(jnp.bfloat16),
        new_values,
        preferred_element_type=jnp.float32,
    )
    weighted = weighted + jnp.einsum(
        "qhk,khd->qhd",
        old_probs.astype(jnp.bfloat16),
        cache_values,
        preferred_element_type=jnp.float32,
    )
    attended = (
        (weighted / denominator[..., None])
        .astype(jnp.bfloat16)
        .reshape(tokens_here, heads_here * HD)
    )
    projected = jnp.dot(attended, w_out, preferred_element_type=jnp.float32)
    attn_share = lax.psum_scatter(projected, "grp", scatter_dimension=1, tiled=True)
    after_cols = (resid.astype(jnp.float32) + attn_share).astype(jnp.bfloat16)
    after_full = lax.all_gather(after_cols, "grp", axis=1, tiled=True)
    after_wide = after_full.astype(jnp.float32)
    squares = jnp.sum(after_wide * after_wide, axis=1)
    inverse = lax.rsqrt(squares / D + EPS)
    normed_full = (
        after_wide * inverse[:, None] * norm_gain.astype(jnp.float32)[None, :]
    ).astype(jnp.bfloat16)
    normed_cols = lax.dynamic_slice_in_dim(normed_full, column_start, column_width, 1)
    logits = jnp.dot(normed_full, w_router, preferred_element_type=jnp.float32)
    route_hits = routes[:, :, None] == jnp.arange(experts_all, dtype=jnp.int32)[None, None, :]
    chosen = jnp.sum(jnp.where(route_hits, logits[:, None, :], 0.0), axis=-1)
    route_weight = jax.nn.softmax(chosen, axis=-1).astype(jnp.bfloat16)
    flat_hits = route_hits.reshape(tokens_here * TOP, experts_all).astype(jnp.int32)
    earlier = jnp.cumsum(flat_hits, axis=0) - flat_hits
    slot_index = jnp.sum(earlier * flat_hits, axis=1)
    slot_row = (routes.reshape(-1) * capacity + slot_index).reshape(tokens_here, TOP)
    slot_ids = jnp.arange(experts_all * capacity, dtype=jnp.int32)
    matches = slot_row[:, :, None] == slot_ids[None, None, :]
    selection = jnp.any(matches, axis=1).astype(jnp.bfloat16)
    combine = jnp.sum(
        jnp.where(matches, route_weight[:, :, None].astype(jnp.float32), 0.0), axis=1
    )
    outgoing = jnp.einsum(
        "tj,td->jd", selection, normed_cols, preferred_element_type=jnp.float32
    ).astype(jnp.bfloat16)
    outgoing = outgoing.reshape(lax.axis_size("ez"), lax.axis_size("ey"), capacity, column_width)
    arrived = lax.all_to_all(outgoing, "ey", split_axis=1, concat_axis=1, tiled=True)
    arrived = lax.all_to_all(arrived, "ez", split_axis=0, concat_axis=0, tiled=True)
    arrived = arrived.reshape(experts_all * capacity, column_width)
    groups = lax.axis_size("grp")
    gathered = lax.all_gather(arrived, "grp", axis=0, tiled=False)
    slice_out = expert_ffn(gathered, w_gate_up[0], w_down[0])
    expert_out = lax.psum_scatter(slice_out, "grp", scatter_dimension=0, tiled=True)
    expert_out = expert_out.reshape(
        lax.axis_size("ez"), lax.axis_size("ey"), capacity, column_width
    )
    returned = lax.all_to_all(expert_out, "ez", split_axis=0, concat_axis=0, tiled=True)
    returned = lax.all_to_all(returned, "ey", split_axis=1, concat_axis=1, tiled=True)
    mixed_cols = jnp.dot(
        combine,
        returned.reshape(experts_all * capacity, column_width),
        precision=lax.Precision.HIGHEST,
        preferred_element_type=jnp.float32,
    )
    return (after_cols, mixed_cols.astype(jnp.bfloat16))


EP = ("ez", "ey")


def solution(mesh):
    grp_size, ep_size = mesh.devices.shape
    side = math.isqrt(ep_size)
    fine = Mesh(mesh.devices.reshape(grp_size, ep_size // side, side), ("grp", "ez", "ey"))
    return jax.shard_map(
        body,
        mesh=fine,
        in_specs=(
            P(EP, "grp"),
            P(EP, "grp"),
            P(EP, "grp"),
            P(EP, "grp"),
            P(None, EP, "grp"),
            P(),
            P("grp", None),
            P(),
            P(),
            P(EP, None),
            P(EP, None, None, "grp"),
            P(EP, "grp", None),
        ),
        out_specs=(P(EP, "grp"), P(EP, "grp")),
        check_vma=False,
    )
```

```python
import jax
import jax.numpy as jnp
from jax import lax
from jax.experimental import pallas as pl
from jax.experimental.pallas import tpu as pltpu
from jax.sharding import PartitionSpec as P

D = 2048
HD = 128
TOP = 4


EPS = 1e-06
MASKED = -1e30


def attention_kernel(len_ref, q_ref, kn_ref, vn_ref, cache_ref, wout_ref, out_ref):
    tokens, width = q_ref.shape
    cache_rows = cache_ref.shape[1]
    length = len_ref[0]
    score_scale = float(HD) ** (-0.5)
    contract_last = (((1,), (1,)), ((), ()))
    causal = lax.broadcasted_iota(jnp.int32, (tokens, tokens), 0) >= lax.broadcasted_iota(
        jnp.int32, (tokens, tokens), 1
    )
    live = lax.broadcasted_iota(jnp.int32, (tokens, cache_rows), 1) < length
    heads = []
    for h in range(width // HD):
        cols = slice(h * HD, (h + 1) * HD)
        q = q_ref[:, cols]
        new_scores = (
            lax.dot_general(q, kn_ref[:, cols], contract_last, preferred_element_type=jnp.float32)
            * score_scale
        )
        new_scores = jnp.where(causal, new_scores, MASKED)
        old_scores = (
            lax.dot_general(
                q, cache_ref[0, :, cols], contract_last, preferred_element_type=jnp.float32
            )
            * score_scale
        )
        old_scores = jnp.where(live, old_scores, MASKED)
        row_max = jnp.maximum(
            jnp.max(new_scores, axis=1, keepdims=True), jnp.max(old_scores, axis=1, keepdims=True)
        )
        new_probs = jnp.exp(new_scores - row_max)
        old_probs = jnp.exp(old_scores - row_max)
        denominator = jnp.sum(new_probs, axis=1, keepdims=True) + jnp.sum(
            old_probs, axis=1, keepdims=True
        )
        weighted = jnp.dot(
            new_probs.astype(jnp.bfloat16), vn_ref[:, cols], preferred_element_type=jnp.float32
        ) + jnp.dot(
            old_probs.astype(jnp.bfloat16), cache_ref[1, :, cols], preferred_element_type=jnp.float32
        )
        heads.append((weighted / denominator).astype(jnp.bfloat16))
    attended = jnp.concatenate(heads, axis=1)
    out_ref[...] = jnp.dot(attended, wout_ref[...], preferred_element_type=jnp.float32)


def attention_projected(own_length, query, key_new, value_new, cache_kv, w_out):
    tokens = query.shape[0]
    whole = lambda shape: pl.BlockSpec(shape, lambda i: (0,) * len(shape))
    return pl.pallas_call(
        attention_kernel,
        grid=(1,),
        in_specs=[
            pl.BlockSpec(memory_space=pltpu.SMEM),
            whole(query.shape),
            whole(key_new.shape),
            whole(value_new.shape),
            whole(cache_kv.shape),
            whole(w_out.shape),
        ],
        out_specs=whole((tokens, w_out.shape[1])),
        out_shape=jax.ShapeDtypeStruct((tokens, w_out.shape[1]), jnp.float32),
    )(own_length, query, key_new, value_new, cache_kv, w_out)


def ffn_kernel(x_ref, gu_ref, down_ref, out_ref):
    groups, rows, width = x_ref.shape
    gate = jnp.zeros((rows, gu_ref.shape[-1]), jnp.float32)
    up = jnp.zeros((rows, gu_ref.shape[-1]), jnp.float32)
    for g in range(groups):
        x = x_ref[g]
        gate = gate + jnp.dot(
            x, gu_ref[0, g * width:(g + 1) * width, :], preferred_element_type=jnp.float32
        )
        up = up + jnp.dot(
            x, gu_ref[1, g * width:(g + 1) * width, :], preferred_element_type=jnp.float32
        )
    hidden = (jax.nn.silu(gate) * up).astype(jnp.bfloat16)
    for g in range(groups):
        out_ref[g] = jnp.dot(
            hidden, down_ref[:, g * width:(g + 1) * width], preferred_element_type=jnp.float32
        ).astype(out_ref.dtype)


def expert_ffn(gathered, gate_up, down, row_tile=256):
    groups, rows, width = gathered.shape
    return pl.pallas_call(
        ffn_kernel,
        grid=(rows // row_tile,),
        in_specs=[
            pl.BlockSpec((groups, row_tile, width), lambda i: (0, i, 0)),
            pl.BlockSpec(gate_up.shape, lambda i: (0, 0, 0)),
            pl.BlockSpec(down.shape, lambda i: (0, 0)),
        ],
        out_specs=pl.BlockSpec((groups, row_tile, width), lambda i: (0, i, 0)),
        out_shape=jax.ShapeDtypeStruct(gathered.shape, jnp.bfloat16),
    )(gathered, gate_up, down)


def body(
    resid,
    query,
    key_new,
    value_new,
    cache_kv,
    cache_len,
    w_out,
    norm_gain,
    w_router,
    routes,
    w_gate_up,
    w_down,
):
    tokens_here = query.shape[0]
    heads_here = query.shape[1] // HD
    experts_all = w_router.shape[1]
    column_width = resid.shape[1]
    group_index = lax.axis_index("grp")
    request = lax.axis_index("ep")
    capacity = max(2, 8 * tokens_here // lax.axis_size("ep"))
    score_scale = float(HD) ** (-0.5)
    column_start = group_index * column_width
    own_length = lax.dynamic_slice_in_dim(cache_len, request, 1, 0)
    projected = attention_projected(own_length, query, key_new, value_new, cache_kv, w_out)
    attn_share = lax.psum_scatter(projected, "grp", scatter_dimension=1, tiled=True)
    after_cols = (resid.astype(jnp.float32) + attn_share).astype(jnp.bfloat16)
    after_full = lax.all_gather(after_cols, "grp", axis=1, tiled=True)
    after_wide = after_full.astype(jnp.float32)
    squares = jnp.sum(after_wide * after_wide, axis=1)
    inverse = lax.rsqrt(squares / D + EPS)
    normed_full = (
        after_wide * inverse[:, None] * norm_gain.astype(jnp.float32)[None, :]
    ).astype(jnp.bfloat16)
    normed_cols = lax.dynamic_slice_in_dim(normed_full, column_start, column_width, 1)
    logits = jnp.dot(normed_full, w_router, preferred_element_type=jnp.float32)
    route_hits = routes[:, :, None] == jnp.arange(experts_all, dtype=jnp.int32)[None, None, :]
    chosen = jnp.sum(jnp.where(route_hits, logits[:, None, :], 0.0), axis=-1)
    route_weight = jax.nn.softmax(chosen, axis=-1).astype(jnp.bfloat16)
    flat_hits = route_hits.reshape(tokens_here * TOP, experts_all).astype(jnp.int32)
    earlier = jnp.cumsum(flat_hits, axis=0) - flat_hits
    slot_index = jnp.sum(earlier * flat_hits, axis=1)
    slot_row = (routes.reshape(-1) * capacity + slot_index).reshape(tokens_here, TOP)
    slot_ids = jnp.arange(experts_all * capacity, dtype=jnp.int32)
    matches = slot_row[:, :, None] == slot_ids[None, None, :]
    selection = jnp.any(matches, axis=1).astype(jnp.bfloat16)
    combine = jnp.sum(
        jnp.where(matches, route_weight[:, :, None].astype(jnp.float32), 0.0), axis=1
    )
    outgoing = jnp.einsum(
        "tj,td->jd", selection, normed_cols, preferred_element_type=jnp.float32
    ).astype(jnp.bfloat16)
    outgoing = outgoing.reshape(experts_all, capacity, column_width)
    arrived = lax.all_to_all(outgoing, "ep", split_axis=0, concat_axis=0, tiled=True)
    arrived = arrived.reshape(experts_all * capacity, column_width)
    groups = lax.axis_size("grp")
    gathered = lax.all_gather(arrived, "grp", axis=0, tiled=False)
    slice_out = expert_ffn(gathered, w_gate_up[0], w_down[0])
    expert_out = lax.psum_scatter(slice_out, "grp", scatter_dimension=0, tiled=True)
    expert_out = expert_out.reshape(experts_all, capacity, column_width)
    returned = lax.all_to_all(expert_out, "ep", split_axis=0, concat_axis=0, tiled=True)
    mixed_cols = jnp.dot(
        combine,
        returned.reshape(experts_all * capacity, column_width),
        precision=lax.Precision.HIGHEST,
        preferred_element_type=jnp.float32,
    )
    return (after_cols, mixed_cols.astype(jnp.bfloat16))


def solution(mesh):
    return jax.shard_map(
        body,
        mesh=mesh,
        in_specs=(
            P("ep", "grp"),
            P("ep", "grp"),
            P("ep", "grp"),
            P("ep", "grp"),
            P(None, "ep", "grp"),
            P(),
            P("grp", None),
            P(),
            P(),
            P("ep", None),
            P("ep", None, None, "grp"),
            P("ep", "grp", None),
        ),
        out_specs=(P("ep", "grp"), P("ep", "grp")),
        check_vma=False,
    )
```

```python
import jax
import jax.numpy as jnp
from jax import lax
from jax.experimental import pallas as pl
from jax.experimental.pallas import tpu as pltpu
from jax.sharding import PartitionSpec as P

D = 2048
HD = 128
TOP = 4


EPS = 1e-06
MASKED = -1e30


def attention_kernel(len_ref, q_ref, kn_ref, vn_ref, cache_ref, out_ref):
    tokens, width = q_ref.shape
    cache_rows = cache_ref.shape[1]
    length = len_ref[lax.axis_index("ep")]
    score_scale = float(HD) ** (-0.5)
    contract_last = (((1,), (1,)), ((), ()))
    causal = lax.broadcasted_iota(jnp.int32, (tokens, tokens), 0) >= lax.broadcasted_iota(
        jnp.int32, (tokens, tokens), 1
    )
    live = lax.broadcasted_iota(jnp.int32, (tokens, cache_rows), 1) < length
    heads = []
    for h in range(width // HD):
        cols = slice(h * HD, (h + 1) * HD)
        q = q_ref[:, cols]
        new_scores = (
            lax.dot_general(q, kn_ref[:, cols], contract_last, preferred_element_type=jnp.float32)
            * score_scale
        )
        new_scores = jnp.where(causal, new_scores, MASKED)
        old_scores = (
            lax.dot_general(
                q, cache_ref[0, :, cols], contract_last, preferred_element_type=jnp.float32
            )
            * score_scale
        )
        old_scores = jnp.where(live, old_scores, MASKED)
        row_max = jnp.maximum(
            jnp.max(new_scores, axis=1, keepdims=True), jnp.max(old_scores, axis=1, keepdims=True)
        )
        new_probs = jnp.exp(new_scores - row_max)
        old_probs = jnp.exp(old_scores - row_max)
        denominator = jnp.sum(new_probs, axis=1, keepdims=True) + jnp.sum(
            old_probs, axis=1, keepdims=True
        )
        weighted = jnp.dot(
            new_probs.astype(jnp.bfloat16), vn_ref[:, cols], preferred_element_type=jnp.float32
        ) + jnp.dot(
            old_probs.astype(jnp.bfloat16), cache_ref[1, :, cols], preferred_element_type=jnp.float32
        )
        heads.append((weighted / denominator).astype(jnp.bfloat16))
    out_ref[...] = jnp.concatenate(heads, axis=1)


def attention(cache_len, query, key_new, value_new, cache_kv):
    whole = lambda shape: pl.BlockSpec(shape, lambda i: (0,) * len(shape))
    return pl.pallas_call(
        attention_kernel,
        grid=(1,),
        in_specs=[
            pl.BlockSpec(memory_space=pltpu.SMEM),
            whole(query.shape),
            whole(key_new.shape),
            whole(value_new.shape),
            whole(cache_kv.shape),
        ],
        out_specs=whole(query.shape),
        out_shape=jax.ShapeDtypeStruct(query.shape, jnp.bfloat16),
    )(cache_len, query, key_new, value_new, cache_kv)


def ffn_kernel(x_ref, gu_ref, down_ref, out_ref):
    groups, rows, width = x_ref.shape
    gate = jnp.zeros((rows, gu_ref.shape[-1]), jnp.float32)
    up = jnp.zeros((rows, gu_ref.shape[-1]), jnp.float32)
    for g in range(groups):
        x = x_ref[g]
        gate = gate + jnp.dot(
            x, gu_ref[0, g * width:(g + 1) * width, :], preferred_element_type=jnp.float32
        )
        up = up + jnp.dot(
            x, gu_ref[1, g * width:(g + 1) * width, :], preferred_element_type=jnp.float32
        )
    hidden = (jax.nn.silu(gate) * up).astype(jnp.bfloat16)
    for g in range(groups):
        out_ref[g] = jnp.dot(
            hidden, down_ref[:, g * width:(g + 1) * width], preferred_element_type=jnp.float32
        ).astype(out_ref.dtype)


def expert_ffn(gathered, gate_up, down, row_tile=256):
    groups, rows, width = gathered.shape
    return pl.pallas_call(
        ffn_kernel,
        grid=(rows // row_tile,),
        in_specs=[
            pl.BlockSpec((groups, row_tile, width), lambda i: (0, i, 0)),
            pl.BlockSpec(gate_up.shape, lambda i: (0, 0, 0)),
            pl.BlockSpec(down.shape, lambda i: (0, 0)),
        ],
        out_specs=pl.BlockSpec((groups, row_tile, width), lambda i: (0, i, 0)),
        out_shape=jax.ShapeDtypeStruct(gathered.shape, jnp.bfloat16),
    )(gathered, gate_up, down)


def body(
    resid,
    query,
    key_new,
    value_new,
    cache_kv,
    cache_len,
    w_out,
    norm_gain,
    w_router,
    routes,
    w_gate_up,
    w_down,
):
    tokens_here = query.shape[0]
    heads_here = query.shape[1] // HD
    experts_all = w_router.shape[1]
    column_width = resid.shape[1]
    group_index = lax.axis_index("grp")
    request = lax.axis_index("ep")
    capacity = max(2, 8 * tokens_here // lax.axis_size("ep"))
    score_scale = float(HD) ** (-0.5)
    column_start = group_index * column_width
    groups = lax.axis_size("grp")
    out_blocks = w_out.reshape(w_out.shape[0], groups, column_width)
    out_cols = lax.all_to_all(out_blocks, "grp", split_axis=1, concat_axis=0, tiled=True)
    out_cols = out_cols.reshape(groups * w_out.shape[0], column_width)
    attended = attention(cache_len, query, key_new, value_new, cache_kv)
    attended_full = lax.all_gather(attended, "grp", axis=1, tiled=True)
    attn_share = jnp.dot(attended_full, out_cols, preferred_element_type=jnp.float32)
    after_cols = (resid.astype(jnp.float32) + attn_share).astype(jnp.bfloat16)
    after_full = lax.all_gather(after_cols, "grp", axis=1, tiled=True)
    after_wide = after_full.astype(jnp.float32)
    squares = jnp.sum(after_wide * after_wide, axis=1)
    inverse = lax.rsqrt(squares / D + EPS)
    normed_full = (
        after_wide * inverse[:, None] * norm_gain.astype(jnp.float32)[None, :]
    ).astype(jnp.bfloat16)
    normed_cols = lax.dynamic_slice_in_dim(normed_full, column_start, column_width, 1)
    logits = jnp.dot(normed_full, w_router, preferred_element_type=jnp.float32)
    route_hits = routes[:, :, None] == jnp.arange(experts_all, dtype=jnp.int32)[None, None, :]
    chosen = jnp.sum(jnp.where(route_hits, logits[:, None, :], 0.0), axis=-1)
    route_weight = jax.nn.softmax(chosen, axis=-1).astype(jnp.bfloat16)
    flat_hits = route_hits.reshape(tokens_here * TOP, experts_all).astype(jnp.int32)
    earlier = jnp.cumsum(flat_hits, axis=0) - flat_hits
    slot_index = jnp.sum(earlier * flat_hits, axis=1)
    slot_row = (routes.reshape(-1) * capacity + slot_index).reshape(tokens_here, TOP)
    slot_ids = jnp.arange(experts_all * capacity, dtype=jnp.int32)
    matches = slot_row[:, :, None] == slot_ids[None, None, :]
    selection = jnp.any(matches, axis=1).astype(jnp.bfloat16)
    combine = jnp.sum(
        jnp.where(matches, route_weight[:, :, None].astype(jnp.float32), 0.0), axis=1
    )
    outgoing = jnp.einsum(
        "tj,td->jd", selection, normed_cols, preferred_element_type=jnp.float32
    ).astype(jnp.bfloat16)
    outgoing = outgoing.reshape(experts_all, capacity, column_width)
    arrived = lax.all_to_all(outgoing, "ep", split_axis=0, concat_axis=0, tiled=True)
    arrived = arrived.reshape(experts_all * capacity, column_width)
    gathered = lax.all_gather(arrived, "grp", axis=0, tiled=False)
    slice_out = expert_ffn(gathered, w_gate_up[0], w_down[0])
    expert_out = lax.psum_scatter(slice_out, "grp", scatter_dimension=0, tiled=True)
    expert_out = expert_out.reshape(experts_all, capacity, column_width)
    returned = lax.all_to_all(expert_out, "ep", split_axis=0, concat_axis=0, tiled=True)
    mixed_cols = jnp.dot(
        combine,
        returned.reshape(experts_all * capacity, column_width),
        precision=lax.Precision.HIGHEST,
        preferred_element_type=jnp.float32,
    )
    return (after_cols, mixed_cols.astype(jnp.bfloat16))


def solution(mesh):
    return jax.shard_map(
        body,
        mesh=mesh,
        in_specs=(
            P("ep", "grp"),
            P("ep", "grp"),
            P("ep", "grp"),
            P("ep", "grp"),
            P(None, "ep", "grp"),
            P(),
            P("grp", None),
            P(),
            P(),
            P("ep", None),
            P("ep", None, None, "grp"),
            P("ep", "grp", None),
        ),
        out_specs=(P("ep", "grp"), P("ep", "grp")),
        check_vma=False,
    )
```

```python
import jax
import jax.numpy as jnp
from jax import lax
from jax.experimental import pallas as pl
from jax.experimental.pallas import tpu as pltpu
from jax.sharding import PartitionSpec as P

D = 2048
HD = 128
TOP = 4


EPS = 1e-06
MASKED = -1e30


def attention_kernel(len_ref, q_ref, kn_ref, vn_ref, cache_ref, out_ref):
    tokens, width = q_ref.shape
    cache_rows = cache_ref.shape[1]
    length = len_ref[lax.axis_index("ep")]
    score_scale = float(HD) ** (-0.5)
    contract_last = (((1,), (1,)), ((), ()))
    causal = lax.broadcasted_iota(jnp.int32, (tokens, tokens), 0) >= lax.broadcasted_iota(
        jnp.int32, (tokens, tokens), 1
    )
    live = lax.broadcasted_iota(jnp.int32, (tokens, cache_rows), 1) < length
    heads = []
    for h in range(width // HD):
        cols = slice(h * HD, (h + 1) * HD)
        q = q_ref[:, cols]
        new_scores = (
            lax.dot_general(q, kn_ref[:, cols], contract_last, preferred_element_type=jnp.float32)
            * score_scale
        )
        new_scores = jnp.where(causal, new_scores, MASKED)
        old_scores = (
            lax.dot_general(
                q, cache_ref[0, :, cols], contract_last, preferred_element_type=jnp.float32
            )
            * score_scale
        )
        old_scores = jnp.where(live, old_scores, MASKED)
        row_max = jnp.maximum(
            jnp.max(new_scores, axis=1, keepdims=True), jnp.max(old_scores, axis=1, keepdims=True)
        )
        new_probs = jnp.exp(new_scores - row_max)
        old_probs = jnp.exp(old_scores - row_max)
        denominator = jnp.sum(new_probs, axis=1, keepdims=True) + jnp.sum(
            old_probs, axis=1, keepdims=True
        )
        weighted = jnp.dot(
            new_probs.astype(jnp.bfloat16), vn_ref[:, cols], preferred_element_type=jnp.float32
        ) + jnp.dot(
            old_probs.astype(jnp.bfloat16), cache_ref[1, :, cols], preferred_element_type=jnp.float32
        )
        heads.append((weighted / denominator).astype(jnp.bfloat16))
    out_ref[...] = jnp.concatenate(heads, axis=1)


def attention(cache_len, query, key_new, value_new, cache_kv):
    whole = lambda shape: pl.BlockSpec(shape, lambda i: (0,) * len(shape))
    return pl.pallas_call(
        attention_kernel,
        grid=(1,),
        in_specs=[
            pl.BlockSpec(memory_space=pltpu.SMEM),
            whole(query.shape),
            whole(key_new.shape),
            whole(value_new.shape),
            whole(cache_kv.shape),
        ],
        out_specs=whole(query.shape),
        out_shape=jax.ShapeDtypeStruct(query.shape, jnp.bfloat16),
    )(cache_len, query, key_new, value_new, cache_kv)


def ffn_kernel(x_ref, gain_ref, gu_ref, down_ref, out_ref):
    groups, rows, width = x_ref.shape
    squares = jnp.zeros((rows, 1), jnp.float32)
    for g in range(groups):
        wide = x_ref[g].astype(jnp.float32)
        squares = squares + jnp.sum(wide * wide, axis=1, keepdims=True)
    inverse = lax.rsqrt(squares / D + EPS)
    gate = jnp.zeros((rows, gu_ref.shape[-1]), jnp.float32)
    up = jnp.zeros((rows, gu_ref.shape[-1]), jnp.float32)
    for g in range(groups):
        x = (x_ref[g].astype(jnp.float32) * inverse * gain_ref[g:g + 1, :]).astype(jnp.bfloat16)
        gate = gate + jnp.dot(
            x, gu_ref[0, g * width:(g + 1) * width, :], preferred_element_type=jnp.float32
        )
        up = up + jnp.dot(
            x, gu_ref[1, g * width:(g + 1) * width, :], preferred_element_type=jnp.float32
        )
    hidden = (jax.nn.silu(gate) * up).astype(jnp.bfloat16)
    for g in range(groups):
        out_ref[g] = jnp.dot(
            hidden, down_ref[:, g * width:(g + 1) * width], preferred_element_type=jnp.float32
        ).astype(out_ref.dtype)


def expert_ffn(gathered, gain_blocks, gate_up, down, row_tile=256):
    groups, rows, width = gathered.shape
    return pl.pallas_call(
        ffn_kernel,
        grid=(rows // row_tile,),
        in_specs=[
            pl.BlockSpec((groups, row_tile, width), lambda i: (0, i, 0)),
            pl.BlockSpec(gain_blocks.shape, lambda i: (0, 0)),
            pl.BlockSpec(gate_up.shape, lambda i: (0, 0, 0)),
            pl.BlockSpec(down.shape, lambda i: (0, 0)),
        ],
        out_specs=pl.BlockSpec((groups, row_tile, width), lambda i: (0, i, 0)),
        out_shape=jax.ShapeDtypeStruct(gathered.shape, jnp.bfloat16),
    )(gathered, gain_blocks, gate_up, down)


def body(
    resid,
    query,
    key_new,
    value_new,
    cache_kv,
    cache_len,
    w_out,
    norm_gain,
    w_router,
    routes,
    w_gate_up,
    w_down,
):
    tokens_here = query.shape[0]
    heads_here = query.shape[1] // HD
    experts_all = w_router.shape[1]
    column_width = resid.shape[1]
    group_index = lax.axis_index("grp")
    request = lax.axis_index("ep")
    capacity = max(2, 8 * tokens_here // lax.axis_size("ep"))
    score_scale = float(HD) ** (-0.5)
    column_start = group_index * column_width
    groups = lax.axis_size("grp")
    out_blocks = w_out.reshape(w_out.shape[0], groups, column_width)
    out_cols = lax.all_to_all(out_blocks, "grp", split_axis=1, concat_axis=0, tiled=True)
    out_cols = out_cols.reshape(groups * w_out.shape[0], column_width)
    attended = attention(cache_len, query, key_new, value_new, cache_kv)
    attended_full = lax.all_gather(attended, "grp", axis=1, tiled=True)
    attn_share = jnp.dot(attended_full, out_cols, preferred_element_type=jnp.float32)
    after_cols = (resid.astype(jnp.float32) + attn_share).astype(jnp.bfloat16)
    after_full = lax.all_gather(after_cols, "grp", axis=1, tiled=True)
    after_wide = after_full.astype(jnp.float32)
    squares = jnp.sum(after_wide * after_wide, axis=1)
    inverse = lax.rsqrt(squares / D + EPS)
    normed_full = (
        after_wide * inverse[:, None] * norm_gain.astype(jnp.float32)[None, :]
    ).astype(jnp.bfloat16)
    logits = jnp.dot(normed_full, w_router, preferred_element_type=jnp.float32)
    route_hits = routes[:, :, None] == jnp.arange(experts_all, dtype=jnp.int32)[None, None, :]
    chosen = jnp.sum(jnp.where(route_hits, logits[:, None, :], 0.0), axis=-1)
    route_weight = jax.nn.softmax(chosen, axis=-1).astype(jnp.bfloat16)
    flat_hits = route_hits.reshape(tokens_here * TOP, experts_all).astype(jnp.int32)
    earlier = jnp.cumsum(flat_hits, axis=0) - flat_hits
    slot_index = jnp.sum(earlier * flat_hits, axis=1)
    slot_row = (routes.reshape(-1) * capacity + slot_index).reshape(tokens_here, TOP)
    slot_ids = jnp.arange(experts_all * capacity, dtype=jnp.int32)
    matches = slot_row[:, :, None] == slot_ids[None, None, :]
    selection = jnp.any(matches, axis=1).astype(jnp.bfloat16)
    combine = jnp.sum(
        jnp.where(matches, route_weight[:, :, None].astype(jnp.float32), 0.0), axis=1
    )
    outgoing = jnp.einsum(
        "tj,td->jd", selection, after_cols, preferred_element_type=jnp.float32
    ).astype(jnp.bfloat16)
    outgoing = outgoing.reshape(experts_all, capacity, column_width)
    arrived = lax.all_to_all(outgoing, "ep", split_axis=0, concat_axis=0, tiled=True)
    arrived = arrived.reshape(experts_all * capacity, column_width)
    gathered = lax.all_gather(arrived, "grp", axis=0, tiled=False)
    gain_blocks = norm_gain.astype(jnp.float32).reshape(groups, column_width)
    slice_out = expert_ffn(gathered, gain_blocks, w_gate_up[0], w_down[0])
    expert_out = lax.psum_scatter(slice_out, "grp", scatter_dimension=0, tiled=True)
    expert_out = expert_out.reshape(experts_all, capacity, column_width)
    returned = lax.all_to_all(expert_out, "ep", split_axis=0, concat_axis=0, tiled=True)
    mixed_cols = jnp.dot(
        combine,
        returned.reshape(experts_all * capacity, column_width),
        precision=lax.Precision.HIGHEST,
        preferred_element_type=jnp.float32,
    )
    return (after_cols, mixed_cols.astype(jnp.bfloat16))


def solution(mesh):
    return jax.shard_map(
        body,
        mesh=mesh,
        in_specs=(
            P("ep", "grp"),
            P("ep", "grp"),
            P("ep", "grp"),
            P("ep", "grp"),
            P(None, "ep", "grp"),
            P(),
            P("grp", None),
            P(),
            P(),
            P("ep", None),
            P("ep", None, None, "grp"),
            P("ep", "grp", None),
        ),
        out_specs=(P("ep", "grp"), P("ep", "grp")),
        check_vma=False,
    )
```

```python
import jax
import jax.numpy as jnp
from jax import lax
from jax.experimental import pallas as pl
from jax.experimental.pallas import tpu as pltpu
from jax.sharding import PartitionSpec as P

D = 2048
HD = 128
TOP = 4


EPS = 1e-06
MASKED = -1e30


def attention_kernel(len_ref, q_ref, kn_ref, vn_ref, cache_ref, out_ref):
    tokens, width = q_ref.shape
    cache_rows = cache_ref.shape[1]
    length = len_ref[lax.axis_index("ep")]
    score_scale = float(HD) ** (-0.5)
    contract_last = (((1,), (1,)), ((), ()))
    causal = lax.broadcasted_iota(jnp.int32, (tokens, tokens), 0) >= lax.broadcasted_iota(
        jnp.int32, (tokens, tokens), 1
    )
    live = lax.broadcasted_iota(jnp.int32, (tokens, cache_rows), 1) < length
    heads = []
    for h in range(width // HD):
        cols = slice(h * HD, (h + 1) * HD)
        q = q_ref[:, cols]
        new_scores = (
            lax.dot_general(q, kn_ref[:, cols], contract_last, preferred_element_type=jnp.float32)
            * score_scale
        )
        new_scores = jnp.where(causal, new_scores, MASKED)
        old_scores = (
            lax.dot_general(
                q, cache_ref[0, :, cols], contract_last, preferred_element_type=jnp.float32
            )
            * score_scale
        )
        old_scores = jnp.where(live, old_scores, MASKED)
        row_max = jnp.maximum(
            jnp.max(new_scores, axis=1, keepdims=True), jnp.max(old_scores, axis=1, keepdims=True)
        )
        new_probs = jnp.exp(new_scores - row_max)
        old_probs = jnp.exp(old_scores - row_max)
        denominator = jnp.sum(new_probs, axis=1, keepdims=True) + jnp.sum(
            old_probs, axis=1, keepdims=True
        )
        weighted = jnp.dot(
            new_probs.astype(jnp.bfloat16), vn_ref[:, cols], preferred_element_type=jnp.float32
        ) + jnp.dot(
            old_probs.astype(jnp.bfloat16), cache_ref[1, :, cols], preferred_element_type=jnp.float32
        )
        heads.append((weighted / denominator).astype(jnp.bfloat16))
    out_ref[...] = jnp.concatenate(heads, axis=1)


def attention(cache_len, query, key_new, value_new, cache_kv):
    whole = lambda shape: pl.BlockSpec(shape, lambda i: (0,) * len(shape))
    return pl.pallas_call(
        attention_kernel,
        grid=(1,),
        in_specs=[
            pl.BlockSpec(memory_space=pltpu.SMEM),
            whole(query.shape),
            whole(key_new.shape),
            whole(value_new.shape),
            whole(cache_kv.shape),
        ],
        out_specs=whole(query.shape),
        out_shape=jax.ShapeDtypeStruct(query.shape, jnp.bfloat16),
    )(cache_len, query, key_new, value_new, cache_kv)


def blocks_kernel(x_ref, out_ref):
    width = out_ref.shape[-1]
    for j in range(out_ref.shape[0]):
        out_ref[j] = x_ref[:, j * width:(j + 1) * width]


def column_blocks(matrix, groups):
    rows, cols = matrix.shape
    shape = (groups, rows, cols // groups)
    return pl.pallas_call(
        blocks_kernel,
        grid=(1,),
        in_specs=[pl.BlockSpec(matrix.shape, lambda i: (0, 0))],
        out_specs=pl.BlockSpec(shape, lambda i: (0, 0, 0)),
        out_shape=jax.ShapeDtypeStruct(shape, matrix.dtype),
    )(matrix)


def ffn_kernel(x_ref, gain_ref, gu_ref, down_ref, out_ref):
    groups, rows, width = x_ref.shape
    squares = jnp.zeros((rows, 1), jnp.float32)
    for g in range(groups):
        wide = x_ref[g].astype(jnp.float32)
        squares = squares + jnp.sum(wide * wide, axis=1, keepdims=True)
    inverse = lax.rsqrt(squares / D + EPS)
    gate = jnp.zeros((rows, gu_ref.shape[1]), jnp.float32)
    up = jnp.zeros((rows, gu_ref.shape[1]), jnp.float32)
    contract_last = (((1,), (1,)), ((), ()))
    for g in range(groups):
        x = (x_ref[g].astype(jnp.float32) * inverse * gain_ref[g:g + 1, :]).astype(jnp.bfloat16)
        gate = gate + lax.dot_general(
            x, gu_ref[0, :, g * width:(g + 1) * width], contract_last,
            preferred_element_type=jnp.float32,
        )
        up = up + lax.dot_general(
            x, gu_ref[1, :, g * width:(g + 1) * width], contract_last,
            preferred_element_type=jnp.float32,
        )
    hidden = (jax.nn.silu(gate) * up).astype(jnp.bfloat16)
    for g in range(groups):
        out_ref[g] = jnp.dot(
            hidden, down_ref[:, g * width:(g + 1) * width], preferred_element_type=jnp.float32
        ).astype(out_ref.dtype)


def expert_ffn(gathered, gain_blocks, gate_up, down, row_tile=256):
    groups, rows, width = gathered.shape
    return pl.pallas_call(
        ffn_kernel,
        grid=(rows // row_tile,),
        in_specs=[
            pl.BlockSpec((groups, row_tile, width), lambda i: (0, i, 0)),
            pl.BlockSpec(gain_blocks.shape, lambda i: (0, 0)),
            pl.BlockSpec(gate_up.shape, lambda i: (0, 0, 0)),
            pl.BlockSpec(down.shape, lambda i: (0, 0)),
        ],
        out_specs=pl.BlockSpec((groups, row_tile, width), lambda i: (0, i, 0)),
        out_shape=jax.ShapeDtypeStruct(gathered.shape, jnp.bfloat16),
    )(gathered, gain_blocks, gate_up, down)


def body(
    resid,
    query,
    key_new,
    value_new,
    cache_kv,
    cache_len,
    w_out,
    norm_gain,
    w_router,
    routes,
    w_gate_up,
    w_down,
):
    tokens_here = query.shape[0]
    heads_here = query.shape[1] // HD
    experts_all = w_router.shape[1]
    column_width = resid.shape[1]
    group_index = lax.axis_index("grp")
    request = lax.axis_index("ep")
    capacity = max(2, 8 * tokens_here // lax.axis_size("ep"))
    score_scale = float(HD) ** (-0.5)
    column_start = group_index * column_width
    groups = lax.axis_size("grp")
    out_blocks = column_blocks(w_out, groups)
    out_cols = lax.all_to_all(out_blocks, "grp", split_axis=0, concat_axis=0, tiled=True)
    out_cols = out_cols.reshape(groups * w_out.shape[0], column_width)
    attended = attention(cache_len, query, key_new, value_new, cache_kv)
    attended_full = lax.all_gather(attended, "grp", axis=1, tiled=True)
    attn_share = jnp.dot(attended_full, out_cols, preferred_element_type=jnp.float32)
    after_cols = (resid.astype(jnp.float32) + attn_share).astype(jnp.bfloat16)
    after_full = lax.all_gather(after_cols, "grp", axis=1, tiled=True)
    after_wide = after_full.astype(jnp.float32)
    squares = jnp.sum(after_wide * after_wide, axis=1)
    inverse = lax.rsqrt(squares / D + EPS)
    normed_full = (
        after_wide * inverse[:, None] * norm_gain.astype(jnp.float32)[None, :]
    ).astype(jnp.bfloat16)
    logits = jnp.dot(normed_full, w_router, preferred_element_type=jnp.float32)
    route_hits = routes[:, :, None] == jnp.arange(experts_all, dtype=jnp.int32)[None, None, :]
    chosen = jnp.sum(jnp.where(route_hits, logits[:, None, :], 0.0), axis=-1)
    route_weight = jax.nn.softmax(chosen, axis=-1).astype(jnp.bfloat16)
    flat_hits = route_hits.reshape(tokens_here * TOP, experts_all).astype(jnp.int32)
    earlier = jnp.cumsum(flat_hits, axis=0) - flat_hits
    slot_index = jnp.sum(earlier * flat_hits, axis=1)
    slot_row = (routes.reshape(-1) * capacity + slot_index).reshape(tokens_here, TOP)
    slot_ids = jnp.arange(experts_all * capacity, dtype=jnp.int32)
    matches = slot_row[:, :, None] == slot_ids[None, None, :]
    selection = jnp.any(matches, axis=1).astype(jnp.bfloat16)
    combine = jnp.sum(
        jnp.where(matches, route_weight[:, :, None].astype(jnp.float32), 0.0), axis=1
    )
    outgoing = jnp.einsum(
        "tj,td->jd", selection, after_cols, preferred_element_type=jnp.float32
    ).astype(jnp.bfloat16)
    outgoing = outgoing.reshape(experts_all, capacity, column_width)
    arrived = lax.all_to_all(outgoing, "ep", split_axis=0, concat_axis=0, tiled=True)
    arrived = arrived.reshape(experts_all * capacity, column_width)
    gathered = lax.all_gather(arrived, "grp", axis=0, tiled=False)
    gain_blocks = norm_gain.astype(jnp.float32).reshape(groups, column_width)
    slice_out = expert_ffn(gathered, gain_blocks, jnp.swapaxes(w_gate_up[0], 1, 2), w_down[0])
    expert_out = lax.psum_scatter(slice_out, "grp", scatter_dimension=0, tiled=True)
    expert_out = expert_out.reshape(experts_all, capacity, column_width)
    returned = lax.all_to_all(expert_out, "ep", split_axis=0, concat_axis=0, tiled=True)
    mixed_cols = jnp.dot(
        combine,
        returned.reshape(experts_all * capacity, column_width),
        precision=lax.Precision.HIGHEST,
        preferred_element_type=jnp.float32,
    )
    return (after_cols, mixed_cols.astype(jnp.bfloat16))


def solution(mesh):
    return jax.shard_map(
        body,
        mesh=mesh,
        in_specs=(
            P("ep", "grp"),
            P("ep", "grp"),
            P("ep", "grp"),
            P("ep", "grp"),
            P(None, "ep", "grp"),
            P(),
            P("grp", None),
            P(),
            P(),
            P("ep", None),
            P("ep", None, None, "grp"),
            P("ep", "grp", None),
        ),
        out_specs=(P("ep", "grp"), P("ep", "grp")),
        check_vma=False,
    )
```

```python
import functools

import jax
import jax.numpy as jnp
from jax import lax
from jax.experimental import pallas as pl
from jax.experimental.pallas import tpu as pltpu
from jax.sharding import Mesh
from jax.sharding import PartitionSpec as P

D = 2048
HD = 128
TOP = 4


EPS = 1e-06
MASKED = -1e30


def attention_kernel(len_ref, q_ref, kn_ref, vn_ref, cache_ref, out_ref):
    tokens, width = q_ref.shape
    cache_rows = cache_ref.shape[1]
    length = len_ref[lax.axis_index("ep")]
    score_scale = float(HD) ** (-0.5)
    contract_last = (((1,), (1,)), ((), ()))
    causal = lax.broadcasted_iota(jnp.int32, (tokens, tokens), 0) >= lax.broadcasted_iota(
        jnp.int32, (tokens, tokens), 1
    )
    live = lax.broadcasted_iota(jnp.int32, (tokens, cache_rows), 1) < length
    heads = []
    for h in range(width // HD):
        cols = slice(h * HD, (h + 1) * HD)
        q = q_ref[:, cols]
        new_scores = (
            lax.dot_general(q, kn_ref[:, cols], contract_last, preferred_element_type=jnp.float32)
            * score_scale
        )
        new_scores = jnp.where(causal, new_scores, MASKED)
        old_scores = (
            lax.dot_general(
                q, cache_ref[0, :, cols], contract_last, preferred_element_type=jnp.float32
            )
            * score_scale
        )
        old_scores = jnp.where(live, old_scores, MASKED)
        row_max = jnp.maximum(
            jnp.max(new_scores, axis=1, keepdims=True), jnp.max(old_scores, axis=1, keepdims=True)
        )
        new_probs = jnp.exp(new_scores - row_max)
        old_probs = jnp.exp(old_scores - row_max)
        denominator = jnp.sum(new_probs, axis=1, keepdims=True) + jnp.sum(
            old_probs, axis=1, keepdims=True
        )
        weighted = jnp.dot(
            new_probs.astype(jnp.bfloat16), vn_ref[:, cols], preferred_element_type=jnp.float32
        ) + jnp.dot(
            old_probs.astype(jnp.bfloat16), cache_ref[1, :, cols], preferred_element_type=jnp.float32
        )
        heads.append((weighted / denominator).astype(jnp.bfloat16))
    out_ref[...] = jnp.concatenate(heads, axis=1)


def attention(cache_len, query, key_new, value_new, cache_kv):
    whole = lambda shape: pl.BlockSpec(shape, lambda i: (0,) * len(shape))
    return pl.pallas_call(
        attention_kernel,
        grid=(1,),
        in_specs=[
            pl.BlockSpec(memory_space=pltpu.SMEM),
            whole(query.shape),
            whole(key_new.shape),
            whole(value_new.shape),
            whole(cache_kv.shape),
        ],
        out_specs=whole(query.shape),
        out_shape=jax.ShapeDtypeStruct(query.shape, jnp.bfloat16),
    )(cache_len, query, key_new, value_new, cache_kv)


GRP = ("gx", "gc")


def blocks_kernel(x_ref, out_ref):
    width = out_ref.shape[-1]
    for j in range(out_ref.shape[0]):
        out_ref[j] = x_ref[:, j * width:(j + 1) * width]


def column_blocks(matrix, groups):
    rows, cols = matrix.shape
    shape = (groups, rows, cols // groups)
    return pl.pallas_call(
        blocks_kernel,
        grid=(1,),
        in_specs=[pl.BlockSpec(matrix.shape, lambda i: (0, 0))],
        out_specs=pl.BlockSpec(shape, lambda i: (0, 0, 0)),
        out_shape=jax.ShapeDtypeStruct(shape, matrix.dtype),
    )(matrix)


def ffn_kernel(x_ref, gain_ref, gu_ref, down_ref, out_ref, cores):
    groups, rows, width = x_ref.shape
    chips = groups // cores
    block_of = [(i % chips) * cores + i // chips for i in range(groups)]
    squares = jnp.zeros((rows, 1), jnp.float32)
    for g in range(groups):
        wide = x_ref[g].astype(jnp.float32)
        squares = squares + jnp.sum(wide * wide, axis=1, keepdims=True)
    inverse = lax.rsqrt(squares / D + EPS)
    gate = jnp.zeros((rows, gu_ref.shape[1]), jnp.float32)
    up = jnp.zeros((rows, gu_ref.shape[1]), jnp.float32)
    contract_last = (((1,), (1,)), ((), ()))
    for g in range(groups):
        x = (x_ref[g].astype(jnp.float32) * inverse * gain_ref[g:g + 1, :]).astype(jnp.bfloat16)
        gate = gate + lax.dot_general(
            x, gu_ref[0, :, block_of[g] * width:(block_of[g] + 1) * width], contract_last,
            preferred_element_type=jnp.float32,
        )
        up = up + lax.dot_general(
            x, gu_ref[1, :, block_of[g] * width:(block_of[g] + 1) * width], contract_last,
            preferred_element_type=jnp.float32,
        )
    hidden = (jax.nn.silu(gate) * up).astype(jnp.bfloat16)
    for g in range(groups):
        out_ref[g] = jnp.dot(
            hidden,
            down_ref[:, block_of[g] * width:(block_of[g] + 1) * width],
            preferred_element_type=jnp.float32,
        ).astype(out_ref.dtype)


def expert_ffn(gathered, gain_blocks, gate_up, down, cores, row_tile=256):
    groups, rows, width = gathered.shape
    return pl.pallas_call(
        functools.partial(ffn_kernel, cores=cores),
        grid=(rows // row_tile,),
        in_specs=[
            pl.BlockSpec((groups, row_tile, width), lambda i: (0, i, 0)),
            pl.BlockSpec(gain_blocks.shape, lambda i: (0, 0)),
            pl.BlockSpec(gate_up.shape, lambda i: (0, 0, 0)),
            pl.BlockSpec(down.shape, lambda i: (0, 0)),
        ],
        out_specs=pl.BlockSpec((groups, row_tile, width), lambda i: (0, i, 0)),
        out_shape=jax.ShapeDtypeStruct(gathered.shape, jnp.bfloat16),
    )(gathered, gain_blocks, gate_up, down)


def body(
    resid,
    query,
    key_new,
    value_new,
    cache_kv,
    cache_len,
    w_out,
    norm_gain,
    w_router,
    routes,
    w_gate_up,
    w_down,
):
    tokens_here = query.shape[0]
    heads_here = query.shape[1] // HD
    experts_all = w_router.shape[1]
    column_width = resid.shape[1]
    group_index = lax.axis_index("gx") * lax.axis_size("gc") + lax.axis_index("gc")
    request = lax.axis_index("ep")
    capacity = max(2, 8 * tokens_here // lax.axis_size("ep"))
    score_scale = float(HD) ** (-0.5)
    column_start = group_index * column_width
    groups = lax.axis_size("gx") * lax.axis_size("gc")
    out_blocks = column_blocks(w_out, groups)
    out_cols = lax.all_to_all(out_blocks, GRP, split_axis=0, concat_axis=0, tiled=True)
    out_cols = out_cols.reshape(groups * w_out.shape[0], column_width)
    attended = attention(cache_len, query, key_new, value_new, cache_kv)
    attended_full = lax.all_gather(attended, GRP, axis=1, tiled=True)
    attn_share = jnp.dot(attended_full, out_cols, preferred_element_type=jnp.float32)
    after_cols = (resid.astype(jnp.float32) + attn_share).astype(jnp.bfloat16)
    after_full = lax.all_gather(after_cols, GRP, axis=1, tiled=True)
    after_wide = after_full.astype(jnp.float32)
    squares = jnp.sum(after_wide * after_wide, axis=1)
    inverse = lax.rsqrt(squares / D + EPS)
    normed_full = (
        after_wide * inverse[:, None] * norm_gain.astype(jnp.float32)[None, :]
    ).astype(jnp.bfloat16)
    logits = jnp.dot(normed_full, w_router, preferred_element_type=jnp.float32)
    route_hits = routes[:, :, None] == jnp.arange(experts_all, dtype=jnp.int32)[None, None, :]
    chosen = jnp.sum(jnp.where(route_hits, logits[:, None, :], 0.0), axis=-1)
    route_weight = jax.nn.softmax(chosen, axis=-1).astype(jnp.bfloat16)
    flat_hits = route_hits.reshape(tokens_here * TOP, experts_all).astype(jnp.int32)
    earlier = jnp.cumsum(flat_hits, axis=0) - flat_hits
    slot_index = jnp.sum(earlier * flat_hits, axis=1)
    slot_row = (routes.reshape(-1) * capacity + slot_index).reshape(tokens_here, TOP)
    slot_ids = jnp.arange(experts_all * capacity, dtype=jnp.int32)
    matches = slot_row[:, :, None] == slot_ids[None, None, :]
    selection = jnp.any(matches, axis=1).astype(jnp.bfloat16)
    combine = jnp.sum(
        jnp.where(matches, route_weight[:, :, None].astype(jnp.float32), 0.0), axis=1
    )
    outgoing = jnp.einsum(
        "tj,td->jd", selection, after_cols, preferred_element_type=jnp.float32
    ).astype(jnp.bfloat16)
    outgoing = outgoing.reshape(experts_all, capacity, column_width)
    arrived = lax.all_to_all(outgoing, "ep", split_axis=0, concat_axis=0, tiled=True)
    arrived = arrived.reshape(experts_all * capacity, column_width)
    gathered = lax.all_gather(arrived, "gx", axis=0, tiled=False)
    gathered = lax.all_gather(gathered, "gc", axis=0, tiled=False)
    gathered = gathered.reshape(groups, experts_all * capacity, column_width)
    cores = lax.axis_size("gc")
    gain_blocks = norm_gain.astype(jnp.float32).reshape(groups, column_width)
    gain_blocks = gain_blocks.reshape(groups // cores, cores, column_width)
    gain_blocks = jnp.swapaxes(gain_blocks, 0, 1).reshape(groups, column_width)
    slice_out = expert_ffn(
        gathered, gain_blocks, jnp.swapaxes(w_gate_up[0], 1, 2), w_down[0], cores
    )
    slice_out = slice_out.reshape(cores, groups // cores, experts_all * capacity, column_width)
    expert_out = lax.psum_scatter(slice_out, "gc", scatter_dimension=0, tiled=True)
    expert_out = lax.psum_scatter(expert_out, "gx", scatter_dimension=1, tiled=True)
    expert_out = expert_out.reshape(experts_all, capacity, column_width)
    returned = lax.all_to_all(expert_out, "ep", split_axis=0, concat_axis=0, tiled=True)
    mixed_cols = jnp.dot(
        combine,
        returned.reshape(experts_all * capacity, column_width),
        precision=lax.Precision.HIGHEST,
        preferred_element_type=jnp.float32,
    )
    return (after_cols, mixed_cols.astype(jnp.bfloat16))


def solution(mesh):
    grp_size, ep_size = mesh.devices.shape
    cores = 2
    fine = Mesh(mesh.devices.reshape(grp_size // cores, cores, ep_size), ("gx", "gc", "ep"))
    return jax.shard_map(
        body,
        mesh=fine,
        in_specs=(
            P("ep", GRP),
            P("ep", GRP),
            P("ep", GRP),
            P("ep", GRP),
            P(None, "ep", GRP),
            P(),
            P(GRP, None),
            P(),
            P(),
            P("ep", None),
            P("ep", None, None, GRP),
            P("ep", GRP, None),
        ),
        out_specs=(P("ep", GRP), P("ep", GRP)),
        check_vma=False,
    )
```

```python
import jax
import jax.numpy as jnp
from jax import lax
from jax.experimental import pallas as pl
from jax.experimental.pallas import tpu as pltpu
from jax.sharding import PartitionSpec as P

D = 2048
HD = 128
TOP = 4


EPS = 1e-06
MASKED = -1e30


def attention_kernel(len_ref, q_ref, kn_ref, vn_ref, cache_ref, wout_ref, out_ref, blocks_ref):
    tokens, width = q_ref.shape
    cache_rows = cache_ref.shape[1]
    length = len_ref[lax.axis_index("ep")]
    score_scale = float(HD) ** (-0.5)
    contract_last = (((1,), (1,)), ((), ()))
    causal = lax.broadcasted_iota(jnp.int32, (tokens, tokens), 0) >= lax.broadcasted_iota(
        jnp.int32, (tokens, tokens), 1
    )
    live = lax.broadcasted_iota(jnp.int32, (tokens, cache_rows), 1) < length
    heads = []
    for h in range(width // HD):
        cols = slice(h * HD, (h + 1) * HD)
        q = q_ref[:, cols]
        new_scores = (
            lax.dot_general(q, kn_ref[:, cols], contract_last, preferred_element_type=jnp.float32)
            * score_scale
        )
        new_scores = jnp.where(causal, new_scores, MASKED)
        old_scores = (
            lax.dot_general(
                q, cache_ref[0, :, cols], contract_last, preferred_element_type=jnp.float32
            )
            * score_scale
        )
        old_scores = jnp.where(live, old_scores, MASKED)
        row_max = jnp.maximum(
            jnp.max(new_scores, axis=1, keepdims=True), jnp.max(old_scores, axis=1, keepdims=True)
        )
        new_probs = jnp.exp(new_scores - row_max)
        old_probs = jnp.exp(old_scores - row_max)
        denominator = jnp.sum(new_probs, axis=1, keepdims=True) + jnp.sum(
            old_probs, axis=1, keepdims=True
        )
        weighted = jnp.dot(
            new_probs.astype(jnp.bfloat16), vn_ref[:, cols], preferred_element_type=jnp.float32
        ) + jnp.dot(
            old_probs.astype(jnp.bfloat16), cache_ref[1, :, cols], preferred_element_type=jnp.float32
        )
        heads.append((weighted / denominator).astype(jnp.bfloat16))
    out_ref[...] = jnp.concatenate(heads, axis=1)
    block_width = blocks_ref.shape[-1]
    for j in range(blocks_ref.shape[0]):
        blocks_ref[j] = wout_ref[:, j * block_width:(j + 1) * block_width]


def attention(cache_len, query, key_new, value_new, cache_kv, w_out, groups):
    whole = lambda shape: pl.BlockSpec(shape, lambda i: (0,) * len(shape))
    rows, cols = w_out.shape
    blocks_shape = (groups, rows, cols // groups)
    return pl.pallas_call(
        attention_kernel,
        grid=(1,),
        in_specs=[
            pl.BlockSpec(memory_space=pltpu.SMEM),
            whole(query.shape),
            whole(key_new.shape),
            whole(value_new.shape),
            whole(cache_kv.shape),
            whole(w_out.shape),
        ],
        out_specs=[whole(query.shape), whole(blocks_shape)],
        out_shape=[
            jax.ShapeDtypeStruct(query.shape, jnp.bfloat16),
            jax.ShapeDtypeStruct(blocks_shape, w_out.dtype),
        ],
    )(cache_len, query, key_new, value_new, cache_kv, w_out)


def ffn_kernel(x_ref, gain_ref, gu_ref, down_ref, out_ref):
    groups, rows, width = x_ref.shape
    squares = jnp.zeros((rows, 1), jnp.float32)
    for g in range(groups):
        wide = x_ref[g].astype(jnp.float32)
        squares = squares + jnp.sum(wide * wide, axis=1, keepdims=True)
    inverse = lax.rsqrt(squares / D + EPS)
    gate = jnp.zeros((rows, gu_ref.shape[1]), jnp.float32)
    up = jnp.zeros((rows, gu_ref.shape[1]), jnp.float32)
    contract_last = (((1,), (1,)), ((), ()))
    for g in range(groups):
        x = (x_ref[g].astype(jnp.float32) * inverse * gain_ref[g:g + 1, :]).astype(jnp.bfloat16)
        gate = gate + lax.dot_general(
            x, gu_ref[0, :, g * width:(g + 1) * width], contract_last,
            preferred_element_type=jnp.float32,
        )
        up = up + lax.dot_general(
            x, gu_ref[1, :, g * width:(g + 1) * width], contract_last,
            preferred_element_type=jnp.float32,
        )
    hidden = (jax.nn.silu(gate) * up).astype(jnp.bfloat16)
    for g in range(groups):
        out_ref[g] = jnp.dot(
            hidden, down_ref[:, g * width:(g + 1) * width], preferred_element_type=jnp.float32
        ).astype(out_ref.dtype)


def expert_ffn(gathered, gain_blocks, gate_up, down, row_tile=256):
    groups, rows, width = gathered.shape
    return pl.pallas_call(
        ffn_kernel,
        grid=(rows // row_tile,),
        in_specs=[
            pl.BlockSpec((groups, row_tile, width), lambda i: (0, i, 0)),
            pl.BlockSpec(gain_blocks.shape, lambda i: (0, 0)),
            pl.BlockSpec(gate_up.shape, lambda i: (0, 0, 0)),
            pl.BlockSpec(down.shape, lambda i: (0, 0)),
        ],
        out_specs=pl.BlockSpec((groups, row_tile, width), lambda i: (0, i, 0)),
        out_shape=jax.ShapeDtypeStruct(gathered.shape, jnp.bfloat16),
    )(gathered, gain_blocks, gate_up, down)


def body(
    resid,
    query,
    key_new,
    value_new,
    cache_kv,
    cache_len,
    w_out,
    norm_gain,
    w_router,
    routes,
    w_gate_up,
    w_down,
):
    tokens_here = query.shape[0]
    heads_here = query.shape[1] // HD
    experts_all = w_router.shape[1]
    column_width = resid.shape[1]
    group_index = lax.axis_index("grp")
    request = lax.axis_index("ep")
    capacity = max(2, 8 * tokens_here // lax.axis_size("ep"))
    score_scale = float(HD) ** (-0.5)
    column_start = group_index * column_width
    groups = lax.axis_size("grp")
    attended, out_blocks = attention(cache_len, query, key_new, value_new, cache_kv, w_out, groups)
    out_cols = lax.all_to_all(out_blocks, "grp", split_axis=0, concat_axis=0, tiled=True)
    out_cols = out_cols.reshape(groups * w_out.shape[0], column_width)
    attended_full = lax.all_gather(attended, "grp", axis=1, tiled=True)
    attn_share = jnp.dot(attended_full, out_cols, preferred_element_type=jnp.float32)
    after_cols = (resid.astype(jnp.float32) + attn_share).astype(jnp.bfloat16)
    after_full = lax.all_gather(after_cols, "grp", axis=1, tiled=True)
    after_wide = after_full.astype(jnp.float32)
    squares = jnp.sum(after_wide * after_wide, axis=1)
    inverse = lax.rsqrt(squares / D + EPS)
    normed_full = (
        after_wide * inverse[:, None] * norm_gain.astype(jnp.float32)[None, :]
    ).astype(jnp.bfloat16)
    logits = jnp.dot(normed_full, w_router, preferred_element_type=jnp.float32)
    route_hits = routes[:, :, None] == jnp.arange(experts_all, dtype=jnp.int32)[None, None, :]
    chosen = jnp.sum(jnp.where(route_hits, logits[:, None, :], 0.0), axis=-1)
    route_weight = jax.nn.softmax(chosen, axis=-1).astype(jnp.bfloat16)
    flat_hits = route_hits.reshape(tokens_here * TOP, experts_all).astype(jnp.int32)
    pair_ids = jnp.arange(tokens_here * TOP, dtype=jnp.int32)
    before = (pair_ids[None, :] < pair_ids[:, None]).astype(jnp.bfloat16)
    earlier = jnp.dot(before, flat_hits.astype(jnp.bfloat16), preferred_element_type=jnp.float32)
    slot_index = jnp.sum(earlier * flat_hits.astype(jnp.float32), axis=1).astype(jnp.int32)
    slot_row = (routes.reshape(-1) * capacity + slot_index).reshape(tokens_here, TOP)
    slot_ids = jnp.arange(experts_all * capacity, dtype=jnp.int32)
    matches = slot_row[:, :, None] == slot_ids[None, None, :]
    selection = jnp.any(matches, axis=1).astype(jnp.bfloat16)
    combine = jnp.sum(
        jnp.where(matches, route_weight[:, :, None].astype(jnp.float32), 0.0), axis=1
    )
    outgoing = jnp.einsum(
        "tj,td->jd", selection, after_cols, preferred_element_type=jnp.float32
    ).astype(jnp.bfloat16)
    outgoing = outgoing.reshape(experts_all, capacity, column_width)
    arrived = lax.all_to_all(outgoing, "ep", split_axis=0, concat_axis=0, tiled=True)
    arrived = arrived.reshape(experts_all * capacity, column_width)
    gathered = lax.all_gather(arrived, "grp", axis=0, tiled=False)
    gain_blocks = norm_gain.astype(jnp.float32).reshape(groups, column_width)
    slice_out = expert_ffn(gathered, gain_blocks, jnp.swapaxes(w_gate_up[0], 1, 2), w_down[0])
    expert_out = lax.psum_scatter(slice_out, "grp", scatter_dimension=0, tiled=True)
    expert_out = expert_out.reshape(experts_all, capacity, column_width)
    returned = lax.all_to_all(expert_out, "ep", split_axis=0, concat_axis=0, tiled=True)
    mixed_cols = jnp.dot(
        combine,
        returned.reshape(experts_all * capacity, column_width),
        precision=lax.Precision.HIGHEST,
        preferred_element_type=jnp.float32,
    )
    return (after_cols, mixed_cols.astype(jnp.bfloat16))


def solution(mesh):
    return jax.shard_map(
        body,
        mesh=mesh,
        in_specs=(
            P("ep", "grp"),
            P("ep", "grp"),
            P("ep", "grp"),
            P("ep", "grp"),
            P(None, "ep", "grp"),
            P(),
            P("grp", None),
            P(),
            P(),
            P("ep", None),
            P("ep", None, None, "grp"),
            P("ep", "grp", None),
        ),
        out_specs=(P("ep", "grp"), P("ep", "grp")),
        check_vma=False,
    )
```

```python
import jax
import jax.numpy as jnp
from jax import lax
from jax.experimental import pallas as pl
from jax.experimental.pallas import tpu as pltpu
from jax.sharding import PartitionSpec as P

D = 2048
HD = 128
TOP = 4


EPS = 1e-06
MASKED = -1e30


def attention_kernel(len_ref, q_ref, kn_ref, vn_ref, cache_ref, out_ref):
    tokens, width = q_ref.shape
    cache_rows = cache_ref.shape[1]
    length = len_ref[lax.axis_index("ep")]
    score_scale = float(HD) ** (-0.5)
    contract_last = (((1,), (1,)), ((), ()))
    causal = lax.broadcasted_iota(jnp.int32, (tokens, tokens), 0) >= lax.broadcasted_iota(
        jnp.int32, (tokens, tokens), 1
    )
    live = lax.broadcasted_iota(jnp.int32, (tokens, cache_rows), 1) < length
    heads = []
    for h in range(width // HD):
        cols = slice(h * HD, (h + 1) * HD)
        q = q_ref[:, cols]
        new_scores = (
            lax.dot_general(q, kn_ref[:, cols], contract_last, preferred_element_type=jnp.float32)
            * score_scale
        )
        new_scores = jnp.where(causal, new_scores, MASKED)
        old_scores = (
            lax.dot_general(
                q, cache_ref[0, :, cols], contract_last, preferred_element_type=jnp.float32
            )
            * score_scale
        )
        old_scores = jnp.where(live, old_scores, MASKED)
        row_max = jnp.maximum(
            jnp.max(new_scores, axis=1, keepdims=True), jnp.max(old_scores, axis=1, keepdims=True)
        )
        new_probs = jnp.exp(new_scores - row_max)
        old_probs = jnp.exp(old_scores - row_max)
        denominator = jnp.sum(new_probs, axis=1, keepdims=True) + jnp.sum(
            old_probs, axis=1, keepdims=True
        )
        weighted = jnp.dot(
            new_probs.astype(jnp.bfloat16), vn_ref[:, cols], preferred_element_type=jnp.float32
        ) + jnp.dot(
            old_probs.astype(jnp.bfloat16), cache_ref[1, :, cols], preferred_element_type=jnp.float32
        )
        heads.append((weighted / denominator).astype(jnp.bfloat16))
    out_ref[...] = jnp.concatenate(heads, axis=1)


def attention(cache_len, query, key_new, value_new, cache_kv):
    whole = lambda shape: pl.BlockSpec(shape, lambda i: (0,) * len(shape))
    return pl.pallas_call(
        attention_kernel,
        grid=(1,),
        in_specs=[
            pl.BlockSpec(memory_space=pltpu.SMEM),
            whole(query.shape),
            whole(key_new.shape),
            whole(value_new.shape),
            whole(cache_kv.shape),
        ],
        out_specs=whole(query.shape),
        out_shape=jax.ShapeDtypeStruct(query.shape, jnp.bfloat16),
    )(cache_len, query, key_new, value_new, cache_kv)


def blocks_kernel(x_ref, out_ref):
    width = out_ref.shape[-1]
    for j in range(out_ref.shape[0]):
        out_ref[j] = x_ref[:, j * width:(j + 1) * width]


def column_blocks(matrix, groups):
    rows, cols = matrix.shape
    shape = (groups, rows, cols // groups)
    return pl.pallas_call(
        blocks_kernel,
        grid=(1,),
        in_specs=[pl.BlockSpec(matrix.shape, lambda i: (0, 0))],
        out_specs=pl.BlockSpec(shape, lambda i: (0, 0, 0)),
        out_shape=jax.ShapeDtypeStruct(shape, matrix.dtype),
    )(matrix)


def ffn_kernel(x_ref, gain_ref, gu_ref, down_ref, out_ref):
    groups, rows, width = x_ref.shape
    squares = jnp.zeros((rows, 1), jnp.float32)
    for g in range(groups):
        wide = x_ref[g].astype(jnp.float32)
        squares = squares + jnp.sum(wide * wide, axis=1, keepdims=True)
    inverse = lax.rsqrt(squares / D + EPS)
    gate = jnp.zeros((rows, gu_ref.shape[1]), jnp.float32)
    up = jnp.zeros((rows, gu_ref.shape[1]), jnp.float32)
    contract_last = (((1,), (1,)), ((), ()))
    for g in range(groups):
        x = (x_ref[g].astype(jnp.float32) * inverse * gain_ref[g:g + 1, :]).astype(jnp.bfloat16)
        gate = gate + lax.dot_general(
            x, gu_ref[0, :, g * width:(g + 1) * width], contract_last,
            preferred_element_type=jnp.float32,
        )
        up = up + lax.dot_general(
            x, gu_ref[1, :, g * width:(g + 1) * width], contract_last,
            preferred_element_type=jnp.float32,
        )
    hidden = (jax.nn.silu(gate) * up).astype(jnp.bfloat16)
    for g in range(groups):
        out_ref[g] = jnp.dot(
            hidden, down_ref[:, g * width:(g + 1) * width], preferred_element_type=jnp.float32
        ).astype(out_ref.dtype)


def expert_ffn(gathered, gain_blocks, gate_up, down, row_tile=512):
    groups, rows, width = gathered.shape
    return pl.pallas_call(
        ffn_kernel,
        grid=(rows // row_tile,),
        in_specs=[
            pl.BlockSpec((groups, row_tile, width), lambda i: (0, i, 0)),
            pl.BlockSpec(gain_blocks.shape, lambda i: (0, 0)),
            pl.BlockSpec(gate_up.shape, lambda i: (0, 0, 0)),
            pl.BlockSpec(down.shape, lambda i: (0, 0)),
        ],
        out_specs=pl.BlockSpec((groups, row_tile, width), lambda i: (0, i, 0)),
        out_shape=jax.ShapeDtypeStruct(gathered.shape, jnp.bfloat16),
    )(gathered, gain_blocks, gate_up, down)


def body(
    resid,
    query,
    key_new,
    value_new,
    cache_kv,
    cache_len,
    w_out,
    norm_gain,
    w_router,
    routes,
    w_gate_up,
    w_down,
):
    tokens_here = query.shape[0]
    heads_here = query.shape[1] // HD
    experts_all = w_router.shape[1]
    column_width = resid.shape[1]
    group_index = lax.axis_index("grp")
    request = lax.axis_index("ep")
    capacity = max(2, 8 * tokens_here // lax.axis_size("ep"))
    score_scale = float(HD) ** (-0.5)
    column_start = group_index * column_width
    groups = lax.axis_size("grp")
    out_blocks = column_blocks(w_out, groups)
    out_cols = lax.all_to_all(out_blocks, "grp", split_axis=0, concat_axis=0, tiled=True)
    out_cols = out_cols.reshape(groups * w_out.shape[0], column_width)
    attended = attention(cache_len, query, key_new, value_new, cache_kv)
    attended_full = lax.all_gather(attended, "grp", axis=1, tiled=True)
    attn_share = jnp.dot(attended_full, out_cols, preferred_element_type=jnp.float32)
    after_cols = (resid.astype(jnp.float32) + attn_share).astype(jnp.bfloat16)
    after_full = lax.all_gather(after_cols, "grp", axis=1, tiled=True)
    after_wide = after_full.astype(jnp.float32)
    squares = jnp.sum(after_wide * after_wide, axis=1)
    inverse = lax.rsqrt(squares / D + EPS)
    normed_full = (
        after_wide * inverse[:, None] * norm_gain.astype(jnp.float32)[None, :]
    ).astype(jnp.bfloat16)
    logits = jnp.dot(normed_full, w_router, preferred_element_type=jnp.float32)
    route_hits = routes[:, :, None] == jnp.arange(experts_all, dtype=jnp.int32)[None, None, :]
    chosen = jnp.sum(jnp.where(route_hits, logits[:, None, :], 0.0), axis=-1)
    route_weight = jax.nn.softmax(chosen, axis=-1).astype(jnp.bfloat16)
    flat_hits = route_hits.reshape(tokens_here * TOP, experts_all).astype(jnp.int32)
    pair_ids = jnp.arange(tokens_here * TOP, dtype=jnp.int32)
    before = (pair_ids[None, :] < pair_ids[:, None]).astype(jnp.bfloat16)
    earlier = jnp.dot(before, flat_hits.astype(jnp.bfloat16), preferred_element_type=jnp.float32)
    slot_index = jnp.sum(earlier * flat_hits.astype(jnp.float32), axis=1).astype(jnp.int32)
    slot_row = (routes.reshape(-1) * capacity + slot_index).reshape(tokens_here, TOP)
    slot_ids = jnp.arange(experts_all * capacity, dtype=jnp.int32)
    matches = slot_row[:, :, None] == slot_ids[None, None, :]
    selection = jnp.any(matches, axis=1).astype(jnp.bfloat16)
    combine = jnp.sum(
        jnp.where(matches, route_weight[:, :, None].astype(jnp.float32), 0.0), axis=1
    )
    outgoing = jnp.einsum(
        "tj,td->jd", selection, after_cols, preferred_element_type=jnp.float32
    ).astype(jnp.bfloat16)
    outgoing = outgoing.reshape(experts_all, capacity, column_width)
    arrived = lax.all_to_all(outgoing, "ep", split_axis=0, concat_axis=0, tiled=True)
    arrived = arrived.reshape(experts_all * capacity, column_width)
    gathered = lax.all_gather(arrived, "grp", axis=0, tiled=False)
    gain_blocks = norm_gain.astype(jnp.float32).reshape(groups, column_width)
    slice_out = expert_ffn(gathered, gain_blocks, jnp.swapaxes(w_gate_up[0], 1, 2), w_down[0])
    expert_out = lax.psum_scatter(slice_out, "grp", scatter_dimension=0, tiled=True)
    expert_out = expert_out.reshape(experts_all, capacity, column_width)
    returned = lax.all_to_all(expert_out, "ep", split_axis=0, concat_axis=0, tiled=True)
    mixed_cols = jnp.dot(
        combine,
        returned.reshape(experts_all * capacity, column_width),
        precision=lax.Precision.HIGHEST,
        preferred_element_type=jnp.float32,
    )
    return (after_cols, mixed_cols.astype(jnp.bfloat16))


def solution(mesh):
    return jax.shard_map(
        body,
        mesh=mesh,
        in_specs=(
            P("ep", "grp"),
            P("ep", "grp"),
            P("ep", "grp"),
            P("ep", "grp"),
            P(None, "ep", "grp"),
            P(),
            P("grp", None),
            P(),
            P(),
            P("ep", None),
            P("ep", None, None, "grp"),
            P("ep", "grp", None),
        ),
        out_specs=(P("ep", "grp"), P("ep", "grp")),
        check_vma=False,
    )
```

```python
import jax
import jax.numpy as jnp
from jax import lax
from jax.experimental import pallas as pl
from jax.experimental.pallas import tpu as pltpu
from jax.sharding import PartitionSpec as P

D = 2048
HD = 128
TOP = 4


EPS = 1e-06
MASKED = -1e30


def attention_kernel(len_ref, q_ref, kn_ref, vn_ref, cache_ref, out_ref):
    tokens, width = q_ref.shape
    cache_rows = cache_ref.shape[1]
    length = len_ref[lax.axis_index("ep")]
    score_scale = float(HD) ** (-0.5)
    contract_last = (((1,), (1,)), ((), ()))
    causal = lax.broadcasted_iota(jnp.int32, (tokens, tokens), 0) >= lax.broadcasted_iota(
        jnp.int32, (tokens, tokens), 1
    )
    live = lax.broadcasted_iota(jnp.int32, (tokens, cache_rows), 1) < length
    heads = []
    for h in range(width // HD):
        cols = slice(h * HD, (h + 1) * HD)
        q = q_ref[:, cols]
        new_scores = (
            lax.dot_general(q, kn_ref[:, cols], contract_last, preferred_element_type=jnp.float32)
            * score_scale
        )
        new_scores = jnp.where(causal, new_scores, MASKED)
        old_scores = (
            lax.dot_general(
                q, cache_ref[0, :, cols], contract_last, preferred_element_type=jnp.float32
            )
            * score_scale
        )
        old_scores = jnp.where(live, old_scores, MASKED)
        row_max = jnp.maximum(
            jnp.max(new_scores, axis=1, keepdims=True), jnp.max(old_scores, axis=1, keepdims=True)
        )
        new_probs = jnp.exp(new_scores - row_max)
        old_probs = jnp.exp(old_scores - row_max)
        denominator = jnp.sum(new_probs, axis=1, keepdims=True) + jnp.sum(
            old_probs, axis=1, keepdims=True
        )
        weighted = jnp.dot(
            new_probs.astype(jnp.bfloat16), vn_ref[:, cols], preferred_element_type=jnp.float32
        ) + jnp.dot(
            old_probs.astype(jnp.bfloat16), cache_ref[1, :, cols], preferred_element_type=jnp.float32
        )
        heads.append((weighted / denominator).astype(jnp.bfloat16))
    out_ref[...] = jnp.concatenate(heads, axis=1)


def attention(cache_len, query, key_new, value_new, cache_kv):
    whole = lambda shape: pl.BlockSpec(shape, lambda i: (0,) * len(shape))
    return pl.pallas_call(
        attention_kernel,
        grid=(1,),
        in_specs=[
            pl.BlockSpec(memory_space=pltpu.SMEM),
            whole(query.shape),
            whole(key_new.shape),
            whole(value_new.shape),
            whole(cache_kv.shape),
        ],
        out_specs=whole(query.shape),
        out_shape=jax.ShapeDtypeStruct(query.shape, jnp.bfloat16),
    )(cache_len, query, key_new, value_new, cache_kv)


def blocks_kernel(x_ref, out_ref):
    width = out_ref.shape[-1]
    for j in range(out_ref.shape[0]):
        out_ref[j] = x_ref[:, j * width:(j + 1) * width]


def column_blocks(matrix, groups):
    rows, cols = matrix.shape
    shape = (groups, rows, cols // groups)
    return pl.pallas_call(
        blocks_kernel,
        grid=(1,),
        in_specs=[pl.BlockSpec(matrix.shape, lambda i: (0, 0))],
        out_specs=pl.BlockSpec(shape, lambda i: (0, 0, 0)),
        out_shape=jax.ShapeDtypeStruct(shape, matrix.dtype),
    )(matrix)


def ffn_kernel(x_ref, gain_ref, gu_ref, down_ref, out_ref):
    groups, rows, width = x_ref.shape
    squares = jnp.zeros((rows, 1), jnp.float32)
    for g in range(groups):
        wide = x_ref[g].astype(jnp.float32)
        squares = squares + jnp.sum(wide * wide, axis=1, keepdims=True)
    inverse = lax.rsqrt(squares / D + EPS)
    gate = jnp.zeros((rows, gu_ref.shape[1]), jnp.float32)
    up = jnp.zeros((rows, gu_ref.shape[1]), jnp.float32)
    contract_last = (((1,), (1,)), ((), ()))
    for g in range(groups):
        x = (x_ref[g].astype(jnp.float32) * inverse * gain_ref[g:g + 1, :]).astype(jnp.bfloat16)
        gate = gate + lax.dot_general(
            x, gu_ref[0, :, g * width:(g + 1) * width], contract_last,
            preferred_element_type=jnp.float32,
        )
        up = up + lax.dot_general(
            x, gu_ref[1, :, g * width:(g + 1) * width], contract_last,
            preferred_element_type=jnp.float32,
        )
    hidden = (jax.nn.silu(gate) * up).astype(jnp.bfloat16)
    for g in range(groups):
        out_ref[g] = jnp.dot(
            hidden, down_ref[:, g * width:(g + 1) * width], preferred_element_type=jnp.float32
        ).astype(out_ref.dtype)


def expert_ffn(gathered, gain_blocks, gate_up, down, row_tile=512):
    groups, rows, width = gathered.shape
    return pl.pallas_call(
        ffn_kernel,
        grid=(rows // row_tile,),
        in_specs=[
            pl.BlockSpec((groups, row_tile, width), lambda i: (0, i, 0)),
            pl.BlockSpec(gain_blocks.shape, lambda i: (0, 0)),
            pl.BlockSpec(gate_up.shape, lambda i: (0, 0, 0)),
            pl.BlockSpec(down.shape, lambda i: (0, 0)),
        ],
        out_specs=pl.BlockSpec((groups, row_tile, width), lambda i: (0, i, 0)),
        out_shape=jax.ShapeDtypeStruct(gathered.shape, jnp.bfloat16),
    )(gathered, gain_blocks, gate_up, down)


def body(
    resid,
    query,
    key_new,
    value_new,
    cache_kv,
    cache_len,
    w_out,
    norm_gain,
    w_router,
    routes,
    w_gate_up,
    w_down,
):
    tokens_here = query.shape[0]
    heads_here = query.shape[1] // HD
    experts_all = w_router.shape[1]
    column_width = resid.shape[1]
    group_index = lax.axis_index("grp")
    request = lax.axis_index("ep")
    capacity = max(2, 8 * tokens_here // lax.axis_size("ep"))
    score_scale = float(HD) ** (-0.5)
    column_start = group_index * column_width
    groups = lax.axis_size("grp")
    out_blocks = column_blocks(w_out, groups)
    out_cols = lax.all_to_all(out_blocks, "grp", split_axis=0, concat_axis=0, tiled=True)
    out_cols = out_cols.reshape(groups * w_out.shape[0], column_width)
    attended = attention(cache_len, query, key_new, value_new, cache_kv)
    attended_all = lax.all_gather(attended, "grp", axis=0, tiled=False)
    attn_share = jnp.einsum(
        "gtd,gdc->tc",
        attended_all,
        out_cols.reshape(groups, column_width, column_width),
        preferred_element_type=jnp.float32,
    )
    after_cols = (resid.astype(jnp.float32) + attn_share).astype(jnp.bfloat16)
    after_full = lax.all_gather(after_cols, "grp", axis=1, tiled=True)
    after_wide = after_full.astype(jnp.float32)
    squares = jnp.sum(after_wide * after_wide, axis=1)
    inverse = lax.rsqrt(squares / D + EPS)
    normed_full = (
        after_wide * inverse[:, None] * norm_gain.astype(jnp.float32)[None, :]
    ).astype(jnp.bfloat16)
    logits = jnp.dot(normed_full, w_router, preferred_element_type=jnp.float32)
    route_hits = routes[:, :, None] == jnp.arange(experts_all, dtype=jnp.int32)[None, None, :]
    chosen = jnp.sum(jnp.where(route_hits, logits[:, None, :], 0.0), axis=-1)
    route_weight = jax.nn.softmax(chosen, axis=-1).astype(jnp.bfloat16)
    flat_hits = route_hits.reshape(tokens_here * TOP, experts_all).astype(jnp.int32)
    pair_ids = jnp.arange(tokens_here * TOP, dtype=jnp.int32)
    before = (pair_ids[None, :] < pair_ids[:, None]).astype(jnp.bfloat16)
    earlier = jnp.dot(before, flat_hits.astype(jnp.bfloat16), preferred_element_type=jnp.float32)
    slot_index = jnp.sum(earlier * flat_hits.astype(jnp.float32), axis=1).astype(jnp.int32)
    slot_row = (routes.reshape(-1) * capacity + slot_index).reshape(tokens_here, TOP)
    slot_ids = jnp.arange(experts_all * capacity, dtype=jnp.int32)
    matches = slot_row[:, :, None] == slot_ids[None, None, :]
    selection = jnp.any(matches, axis=1).astype(jnp.bfloat16)
    combine = jnp.sum(
        jnp.where(matches, route_weight[:, :, None].astype(jnp.float32), 0.0), axis=1
    )
    outgoing = jnp.einsum(
        "tj,td->jd", selection, after_cols, preferred_element_type=jnp.float32
    ).astype(jnp.bfloat16)
    outgoing = outgoing.reshape(experts_all, capacity, column_width)
    arrived = lax.all_to_all(outgoing, "ep", split_axis=0, concat_axis=0, tiled=True)
    arrived = arrived.reshape(experts_all * capacity, column_width)
    gathered = lax.all_gather(arrived, "grp", axis=0, tiled=False)
    gain_blocks = norm_gain.astype(jnp.float32).reshape(groups, column_width)
    slice_out = expert_ffn(gathered, gain_blocks, jnp.swapaxes(w_gate_up[0], 1, 2), w_down[0])
    expert_out = lax.psum_scatter(slice_out, "grp", scatter_dimension=0, tiled=True)
    expert_out = expert_out.reshape(experts_all, capacity, column_width)
    returned = lax.all_to_all(expert_out, "ep", split_axis=0, concat_axis=0, tiled=True)
    mixed_cols = jnp.dot(
        combine,
        returned.reshape(experts_all * capacity, column_width),
        precision=lax.Precision.HIGHEST,
        preferred_element_type=jnp.float32,
    )
    return (after_cols, mixed_cols.astype(jnp.bfloat16))


def solution(mesh):
    return jax.shard_map(
        body,
        mesh=mesh,
        in_specs=(
            P("ep", "grp"),
            P("ep", "grp"),
            P("ep", "grp"),
            P("ep", "grp"),
            P(None, "ep", "grp"),
            P(),
            P("grp", None),
            P(),
            P(),
            P("ep", None),
            P("ep", None, None, "grp"),
            P("ep", "grp", None),
        ),
        out_specs=(P("ep", "grp"), P("ep", "grp")),
        check_vma=False,
    )
```

```python
import jax
import jax.numpy as jnp
from jax import lax
from jax.experimental import pallas as pl
from jax.experimental.pallas import tpu as pltpu
from jax.sharding import PartitionSpec as P

D = 2048
HD = 128
TOP = 4


EPS = 1e-06
MASKED = -1e30


def attention_kernel(len_ref, q_ref, kn_ref, vn_ref, cache_ref, out_ref):
    tokens, width = q_ref.shape
    cache_rows = cache_ref.shape[1]
    length = len_ref[lax.axis_index("ep")]
    score_scale = float(HD) ** (-0.5)
    contract_last = (((1,), (1,)), ((), ()))
    causal = lax.broadcasted_iota(jnp.int32, (tokens, tokens), 0) >= lax.broadcasted_iota(
        jnp.int32, (tokens, tokens), 1
    )
    live = lax.broadcasted_iota(jnp.int32, (tokens, cache_rows), 1) < length
    heads = []
    for h in range(width // HD):
        cols = slice(h * HD, (h + 1) * HD)
        q = q_ref[:, cols]
        new_scores = (
            lax.dot_general(q, kn_ref[:, cols], contract_last, preferred_element_type=jnp.float32)
            * score_scale
        )
        new_scores = jnp.where(causal, new_scores, MASKED)
        old_scores = (
            lax.dot_general(
                q, cache_ref[0, :, cols], contract_last, preferred_element_type=jnp.float32
            )
            * score_scale
        )
        old_scores = jnp.where(live, old_scores, MASKED)
        row_max = jnp.maximum(
            jnp.max(new_scores, axis=1, keepdims=True), jnp.max(old_scores, axis=1, keepdims=True)
        )
        new_probs = jnp.exp(new_scores - row_max)
        old_probs = jnp.exp(old_scores - row_max)
        denominator = jnp.sum(new_probs, axis=1, keepdims=True) + jnp.sum(
            old_probs, axis=1, keepdims=True
        )
        weighted = jnp.dot(
            new_probs.astype(jnp.bfloat16), vn_ref[:, cols], preferred_element_type=jnp.float32
        ) + jnp.dot(
            old_probs.astype(jnp.bfloat16), cache_ref[1, :, cols], preferred_element_type=jnp.float32
        )
        heads.append((weighted / denominator).astype(jnp.bfloat16))
    out_ref[...] = jnp.concatenate(heads, axis=1)


def attention(cache_len, query, key_new, value_new, cache_kv):
    whole = lambda shape: pl.BlockSpec(shape, lambda i: (0,) * len(shape))
    return pl.pallas_call(
        attention_kernel,
        grid=(1,),
        in_specs=[
            pl.BlockSpec(memory_space=pltpu.SMEM),
            whole(query.shape),
            whole(key_new.shape),
            whole(value_new.shape),
            whole(cache_kv.shape),
        ],
        out_specs=whole(query.shape),
        out_shape=jax.ShapeDtypeStruct(query.shape, jnp.bfloat16),
    )(cache_len, query, key_new, value_new, cache_kv)


def blocks_kernel(x_ref, out_ref, sems):
    width = out_ref.shape[-1]
    copies = [
        pltpu.make_async_copy(x_ref.at[:, j * width:(j + 1) * width], out_ref.at[j], sems.at[j])
        for j in range(out_ref.shape[0])
    ]
    for copy in copies:
        copy.start()
    for copy in copies:
        copy.wait()


def column_blocks(matrix, groups):
    rows, cols = matrix.shape
    shape = (groups, rows, cols // groups)
    return pl.pallas_call(
        blocks_kernel,
        in_specs=[pl.BlockSpec(memory_space=pl.ANY)],
        out_specs=pl.BlockSpec(memory_space=pl.ANY),
        out_shape=jax.ShapeDtypeStruct(shape, matrix.dtype),
        scratch_shapes=[pltpu.SemaphoreType.DMA((groups,))],
    )(matrix)


def ffn_kernel(x_ref, gain_ref, gu_ref, down_ref, out_ref):
    groups, rows, width = x_ref.shape
    squares = jnp.zeros((rows, 1), jnp.float32)
    for g in range(groups):
        wide = x_ref[g].astype(jnp.float32)
        squares = squares + jnp.sum(wide * wide, axis=1, keepdims=True)
    inverse = lax.rsqrt(squares / D + EPS)
    gate = jnp.zeros((rows, gu_ref.shape[1]), jnp.float32)
    up = jnp.zeros((rows, gu_ref.shape[1]), jnp.float32)
    contract_last = (((1,), (1,)), ((), ()))
    for g in range(groups):
        x = (x_ref[g].astype(jnp.float32) * inverse * gain_ref[g:g + 1, :]).astype(jnp.bfloat16)
        gate = gate + lax.dot_general(
            x, gu_ref[0, :, g * width:(g + 1) * width], contract_last,
            preferred_element_type=jnp.float32,
        )
        up = up + lax.dot_general(
            x, gu_ref[1, :, g * width:(g + 1) * width], contract_last,
            preferred_element_type=jnp.float32,
        )
    hidden = (jax.nn.silu(gate) * up).astype(jnp.bfloat16)
    for g in range(groups):
        out_ref[g] = jnp.dot(
            hidden, down_ref[:, g * width:(g + 1) * width], preferred_element_type=jnp.float32
        ).astype(out_ref.dtype)


def expert_ffn(gathered, gain_blocks, gate_up, down, row_tile=512):
    groups, rows, width = gathered.shape
    return pl.pallas_call(
        ffn_kernel,
        grid=(rows // row_tile,),
        in_specs=[
            pl.BlockSpec((groups, row_tile, width), lambda i: (0, i, 0)),
            pl.BlockSpec(gain_blocks.shape, lambda i: (0, 0)),
            pl.BlockSpec(gate_up.shape, lambda i: (0, 0, 0)),
            pl.BlockSpec(down.shape, lambda i: (0, 0)),
        ],
        out_specs=pl.BlockSpec((groups, row_tile, width), lambda i: (0, i, 0)),
        out_shape=jax.ShapeDtypeStruct(gathered.shape, jnp.bfloat16),
    )(gathered, gain_blocks, gate_up, down)


def body(
    resid,
    query,
    key_new,
    value_new,
    cache_kv,
    cache_len,
    w_out,
    norm_gain,
    w_router,
    routes,
    w_gate_up,
    w_down,
):
    tokens_here = query.shape[0]
    heads_here = query.shape[1] // HD
    experts_all = w_router.shape[1]
    column_width = resid.shape[1]
    group_index = lax.axis_index("grp")
    request = lax.axis_index("ep")
    capacity = max(2, 8 * tokens_here // lax.axis_size("ep"))
    score_scale = float(HD) ** (-0.5)
    column_start = group_index * column_width
    groups = lax.axis_size("grp")
    out_blocks = column_blocks(w_out, groups)
    out_cols = lax.all_to_all(out_blocks, "grp", split_axis=0, concat_axis=0, tiled=True)
    out_cols = out_cols.reshape(groups * w_out.shape[0], column_width)
    attended = attention(cache_len, query, key_new, value_new, cache_kv)
    attended_all = lax.all_gather(attended, "grp", axis=0, tiled=False)
    attn_share = jnp.einsum(
        "gtd,gdc->tc",
        attended_all,
        out_cols.reshape(groups, column_width, column_width),
        preferred_element_type=jnp.float32,
    )
    after_cols = (resid.astype(jnp.float32) + attn_share).astype(jnp.bfloat16)
    after_full = lax.all_gather(after_cols, "grp", axis=1, tiled=True)
    after_wide = after_full.astype(jnp.float32)
    squares = jnp.sum(after_wide * after_wide, axis=1)
    inverse = lax.rsqrt(squares / D + EPS)
    normed_full = (
        after_wide * inverse[:, None] * norm_gain.astype(jnp.float32)[None, :]
    ).astype(jnp.bfloat16)
    logits = jnp.dot(normed_full, w_router, preferred_element_type=jnp.float32)
    route_hits = routes[:, :, None] == jnp.arange(experts_all, dtype=jnp.int32)[None, None, :]
    chosen = jnp.sum(jnp.where(route_hits, logits[:, None, :], 0.0), axis=-1)
    route_weight = jax.nn.softmax(chosen, axis=-1).astype(jnp.bfloat16)
    flat_hits = route_hits.reshape(tokens_here * TOP, experts_all).astype(jnp.int32)
    pair_ids = jnp.arange(tokens_here * TOP, dtype=jnp.int32)
    before = (pair_ids[None, :] < pair_ids[:, None]).astype(jnp.bfloat16)
    earlier = jnp.dot(before, flat_hits.astype(jnp.bfloat16), preferred_element_type=jnp.float32)
    slot_index = jnp.sum(earlier * flat_hits.astype(jnp.float32), axis=1).astype(jnp.int32)
    slot_row = (routes.reshape(-1) * capacity + slot_index).reshape(tokens_here, TOP)
    slot_ids = jnp.arange(experts_all * capacity, dtype=jnp.int32)
    matches = slot_row[:, :, None] == slot_ids[None, None, :]
    selection = jnp.any(matches, axis=1).astype(jnp.bfloat16)
    combine = jnp.sum(
        jnp.where(matches, route_weight[:, :, None].astype(jnp.float32), 0.0), axis=1
    )
    outgoing = jnp.einsum(
        "tj,td->jd", selection, after_cols, preferred_element_type=jnp.float32
    ).astype(jnp.bfloat16)
    outgoing = outgoing.reshape(experts_all, capacity, column_width)
    arrived = lax.all_to_all(outgoing, "ep", split_axis=0, concat_axis=0, tiled=True)
    arrived = arrived.reshape(experts_all * capacity, column_width)
    gathered = lax.all_gather(arrived, "grp", axis=0, tiled=False)
    gain_blocks = norm_gain.astype(jnp.float32).reshape(groups, column_width)
    slice_out = expert_ffn(gathered, gain_blocks, jnp.swapaxes(w_gate_up[0], 1, 2), w_down[0])
    expert_out = lax.psum_scatter(slice_out, "grp", scatter_dimension=0, tiled=True)
    expert_out = expert_out.reshape(experts_all, capacity, column_width)
    returned = lax.all_to_all(expert_out, "ep", split_axis=0, concat_axis=0, tiled=True)
    mixed_cols = jnp.dot(
        combine,
        returned.reshape(experts_all * capacity, column_width),
        precision=lax.Precision.HIGHEST,
        preferred_element_type=jnp.float32,
    )
    return (after_cols, mixed_cols.astype(jnp.bfloat16))


def solution(mesh):
    return jax.shard_map(
        body,
        mesh=mesh,
        in_specs=(
            P("ep", "grp"),
            P("ep", "grp"),
            P("ep", "grp"),
            P("ep", "grp"),
            P(None, "ep", "grp"),
            P(),
            P("grp", None),
            P(),
            P(),
            P("ep", None),
            P("ep", None, None, "grp"),
            P("ep", "grp", None),
        ),
        out_specs=(P("ep", "grp"), P("ep", "grp")),
        check_vma=False,
    )
```

```python
import jax
import jax.numpy as jnp
from jax import lax
from jax.experimental import pallas as pl
from jax.experimental.pallas import tpu as pltpu
from jax.sharding import PartitionSpec as P

D = 2048
HD = 128
TOP = 4


EPS = 1e-06
MASKED = -1e30


def attention_kernel(len_ref, q_ref, kn_ref, vn_ref, cache_ref, out_ref):
    tokens, width = q_ref.shape
    cache_rows = cache_ref.shape[1]
    length = len_ref[lax.axis_index("ep")]
    score_scale = float(HD) ** (-0.5)
    contract_last = (((1,), (1,)), ((), ()))
    causal = lax.broadcasted_iota(jnp.int32, (tokens, tokens), 0) >= lax.broadcasted_iota(
        jnp.int32, (tokens, tokens), 1
    )
    live = lax.broadcasted_iota(jnp.int32, (tokens, cache_rows), 1) < length
    heads = []
    for h in range(width // HD):
        cols = slice(h * HD, (h + 1) * HD)
        q = q_ref[:, cols]
        new_scores = (
            lax.dot_general(q, kn_ref[:, cols], contract_last, preferred_element_type=jnp.float32)
            * score_scale
        )
        new_scores = jnp.where(causal, new_scores, MASKED)
        old_scores = (
            lax.dot_general(
                q, cache_ref[0, :, cols], contract_last, preferred_element_type=jnp.float32
            )
            * score_scale
        )
        old_scores = jnp.where(live, old_scores, MASKED)
        row_max = jnp.maximum(
            jnp.max(new_scores, axis=1, keepdims=True), jnp.max(old_scores, axis=1, keepdims=True)
        )
        new_probs = jnp.exp(new_scores - row_max)
        old_probs = jnp.exp(old_scores - row_max)
        denominator = jnp.sum(new_probs, axis=1, keepdims=True) + jnp.sum(
            old_probs, axis=1, keepdims=True
        )
        weighted = jnp.dot(
            new_probs.astype(jnp.bfloat16), vn_ref[:, cols], preferred_element_type=jnp.float32
        ) + jnp.dot(
            old_probs.astype(jnp.bfloat16), cache_ref[1, :, cols], preferred_element_type=jnp.float32
        )
        heads.append((weighted / denominator).astype(jnp.bfloat16))
    out_ref[...] = jnp.concatenate(heads, axis=1)


def attention(cache_len, query, key_new, value_new, cache_kv):
    whole = lambda shape: pl.BlockSpec(shape, lambda i: (0,) * len(shape))
    return pl.pallas_call(
        attention_kernel,
        grid=(1,),
        in_specs=[
            pl.BlockSpec(memory_space=pltpu.SMEM),
            whole(query.shape),
            whole(key_new.shape),
            whole(value_new.shape),
            whole(cache_kv.shape),
        ],
        out_specs=whole(query.shape),
        out_shape=jax.ShapeDtypeStruct(query.shape, jnp.bfloat16),
    )(cache_len, query, key_new, value_new, cache_kv)


def blocks_kernel(x_ref, out_ref):
    width = out_ref.shape[-1]
    for j in range(out_ref.shape[0]):
        out_ref[j] = x_ref[:, j * width:(j + 1) * width]


def column_blocks(matrix, groups):
    rows, cols = matrix.shape
    shape = (groups, rows, cols // groups)
    return pl.pallas_call(
        blocks_kernel,
        grid=(1,),
        in_specs=[pl.BlockSpec(matrix.shape, lambda i: (0, 0))],
        out_specs=pl.BlockSpec(shape, lambda i: (0, 0, 0)),
        out_shape=jax.ShapeDtypeStruct(shape, matrix.dtype),
    )(matrix)


def ffn_kernel(x_ref, gain_ref, gu_ref, down_ref, out_ref):
    groups, rows, width = x_ref.shape
    squares = jnp.zeros((rows, 1), jnp.float32)
    for g in range(groups):
        wide = x_ref[g].astype(jnp.float32)
        squares = squares + jnp.sum(wide * wide, axis=1, keepdims=True)
    inverse = lax.rsqrt(squares / D + EPS)
    gate = jnp.zeros((rows, gu_ref.shape[1]), jnp.float32)
    up = jnp.zeros((rows, gu_ref.shape[1]), jnp.float32)
    contract_last = (((1,), (1,)), ((), ()))
    for g in range(groups):
        x = (x_ref[g].astype(jnp.float32) * inverse * gain_ref[g:g + 1, :]).astype(jnp.bfloat16)
        gate = gate + lax.dot_general(
            x, gu_ref[0, :, g * width:(g + 1) * width], contract_last,
            preferred_element_type=jnp.float32,
        )
        up = up + lax.dot_general(
            x, gu_ref[1, :, g * width:(g + 1) * width], contract_last,
            preferred_element_type=jnp.float32,
        )
    hidden = (jax.nn.silu(gate) * up).astype(jnp.bfloat16)
    for g in range(groups):
        out_ref[g] = jnp.dot(
            hidden, down_ref[:, g * width:(g + 1) * width], preferred_element_type=jnp.float32
        ).astype(out_ref.dtype)


def expert_ffn(gathered, gain_blocks, gate_up, down, row_tile=512):
    groups, rows, width = gathered.shape
    return pl.pallas_call(
        ffn_kernel,
        grid=(rows // row_tile,),
        in_specs=[
            pl.BlockSpec((groups, row_tile, width), lambda i: (0, i, 0)),
            pl.BlockSpec(gain_blocks.shape, lambda i: (0, 0)),
            pl.BlockSpec(gate_up.shape, lambda i: (0, 0, 0)),
            pl.BlockSpec(down.shape, lambda i: (0, 0)),
        ],
        out_specs=pl.BlockSpec((groups, row_tile, width), lambda i: (0, i, 0)),
        out_shape=jax.ShapeDtypeStruct(gathered.shape, jnp.bfloat16),
    )(gathered, gain_blocks, gate_up, down)


def body(
    resid,
    query,
    key_new,
    value_new,
    cache_kv,
    cache_len,
    w_out,
    norm_gain,
    w_router,
    routes,
    w_gate_up,
    w_down,
):
    tokens_here = query.shape[0]
    heads_here = query.shape[1] // HD
    experts_all = w_router.shape[1]
    column_width = resid.shape[1]
    group_index = lax.axis_index("grp")
    request = lax.axis_index("ep")
    capacity = max(2, 8 * tokens_here // lax.axis_size("ep"))
    score_scale = float(HD) ** (-0.5)
    column_start = group_index * column_width
    groups = lax.axis_size("grp")
    out_blocks = column_blocks(w_out, groups)
    out_cols = lax.all_to_all(out_blocks, "grp", split_axis=0, concat_axis=0, tiled=True)
    out_cols = out_cols.reshape(groups * w_out.shape[0], column_width)
    attended = attention(cache_len, query, key_new, value_new, cache_kv)
    attended_all = lax.all_gather(attended, "grp", axis=0, tiled=False)
    attn_share = jnp.einsum(
        "gtd,gdc->tc",
        attended_all,
        out_cols.reshape(groups, column_width, column_width),
        preferred_element_type=jnp.float32,
    )
    after_cols = (resid.astype(jnp.float32) + attn_share).astype(jnp.bfloat16)
    after_full = lax.all_gather(after_cols, "grp", axis=1, tiled=True)
    after_wide = after_full.astype(jnp.float32)
    squares = jnp.sum(after_wide * after_wide, axis=1)
    inverse = lax.rsqrt(squares / D + EPS)
    normed_full = (
        after_wide * inverse[:, None] * norm_gain.astype(jnp.float32)[None, :]
    ).astype(jnp.bfloat16)
    logits = jnp.dot(normed_full, w_router, preferred_element_type=jnp.float32)
    route_hits = routes[:, :, None] == jnp.arange(experts_all, dtype=jnp.int32)[None, None, :]
    chosen = jnp.sum(jnp.where(route_hits, logits[:, None, :], 0.0), axis=-1)
    route_weight = jax.nn.softmax(chosen, axis=-1).astype(jnp.bfloat16)
    flat_hits = route_hits.reshape(tokens_here * TOP, experts_all).astype(jnp.int32)
    pair_ids = jnp.arange(tokens_here * TOP, dtype=jnp.int32)
    before = (pair_ids[None, :] < pair_ids[:, None]).astype(jnp.bfloat16)
    earlier = jnp.dot(before, flat_hits.astype(jnp.bfloat16), preferred_element_type=jnp.float32)
    slot_index = jnp.sum(earlier * flat_hits.astype(jnp.float32), axis=1).astype(jnp.int32)
    slot_row = (routes.reshape(-1) * capacity + slot_index).reshape(tokens_here, TOP)
    slot_ids = jnp.arange(experts_all * capacity, dtype=jnp.int32)
    matches = slot_row[:, :, None] == slot_ids[None, None, :]
    selection = jnp.any(matches, axis=1).astype(jnp.bfloat16)
    combine = jnp.sum(
        jnp.where(matches, route_weight[:, :, None], jnp.zeros((), jnp.bfloat16)), axis=1
    )
    outgoing = jnp.einsum(
        "tj,td->jd", selection, after_cols, preferred_element_type=jnp.float32
    ).astype(jnp.bfloat16)
    outgoing = outgoing.reshape(experts_all, capacity, column_width)
    arrived = lax.all_to_all(outgoing, "ep", split_axis=0, concat_axis=0, tiled=True)
    arrived = arrived.reshape(experts_all * capacity, column_width)
    gathered = lax.all_gather(arrived, "grp", axis=0, tiled=False)
    gain_blocks = norm_gain.astype(jnp.float32).reshape(groups, column_width)
    slice_out = expert_ffn(gathered, gain_blocks, jnp.swapaxes(w_gate_up[0], 1, 2), w_down[0])
    expert_out = lax.psum_scatter(slice_out, "grp", scatter_dimension=0, tiled=True)
    expert_out = expert_out.reshape(experts_all, capacity, column_width)
    returned = lax.all_to_all(expert_out, "ep", split_axis=0, concat_axis=0, tiled=True)
    mixed_cols = jnp.dot(
        combine,
        returned.reshape(experts_all * capacity, column_width),
        preferred_element_type=jnp.float32,
    )
    return (after_cols, mixed_cols.astype(jnp.bfloat16))


def solution(mesh):
    return jax.shard_map(
        body,
        mesh=mesh,
        in_specs=(
            P("ep", "grp"),
            P("ep", "grp"),
            P("ep", "grp"),
            P("ep", "grp"),
            P(None, "ep", "grp"),
            P(),
            P("grp", None),
            P(),
            P(),
            P("ep", None),
            P("ep", None, None, "grp"),
            P("ep", "grp", None),
        ),
        out_specs=(P("ep", "grp"), P("ep", "grp")),
        check_vma=False,
    )
```

```python
import jax
import jax.numpy as jnp
from jax import lax
from jax.experimental import pallas as pl
from jax.experimental.pallas import tpu as pltpu
from jax.sharding import PartitionSpec as P

D = 2048
HD = 128
TOP = 4


EPS = 1e-06
MASKED = -1e30


def attention_kernel(len_ref, q_ref, kn_ref, vn_ref, cache_ref, wout_ref, out_ref):
    tokens, width = q_ref.shape
    cache_rows = cache_ref.shape[1]
    length = len_ref[lax.axis_index("ep")]
    score_scale = float(HD) ** (-0.5)
    contract_last = (((1,), (1,)), ((), ()))
    causal = lax.broadcasted_iota(jnp.int32, (tokens, tokens), 0) >= lax.broadcasted_iota(
        jnp.int32, (tokens, tokens), 1
    )
    live = lax.broadcasted_iota(jnp.int32, (tokens, cache_rows), 1) < length
    heads = []
    for h in range(width // HD):
        cols = slice(h * HD, (h + 1) * HD)
        q = q_ref[:, cols]
        new_scores = (
            lax.dot_general(q, kn_ref[:, cols], contract_last, preferred_element_type=jnp.float32)
            * score_scale
        )
        new_scores = jnp.where(causal, new_scores, MASKED)
        old_scores = (
            lax.dot_general(
                q, cache_ref[0, :, cols], contract_last, preferred_element_type=jnp.float32
            )
            * score_scale
        )
        old_scores = jnp.where(live, old_scores, MASKED)
        row_max = jnp.maximum(
            jnp.max(new_scores, axis=1, keepdims=True), jnp.max(old_scores, axis=1, keepdims=True)
        )
        new_probs = jnp.exp(new_scores - row_max)
        old_probs = jnp.exp(old_scores - row_max)
        denominator = jnp.sum(new_probs, axis=1, keepdims=True) + jnp.sum(
            old_probs, axis=1, keepdims=True
        )
        weighted = jnp.dot(
            new_probs.astype(jnp.bfloat16), vn_ref[:, cols], preferred_element_type=jnp.float32
        ) + jnp.dot(
            old_probs.astype(jnp.bfloat16), cache_ref[1, :, cols], preferred_element_type=jnp.float32
        )
        heads.append((weighted / denominator).astype(jnp.bfloat16))
    attended = jnp.concatenate(heads, axis=1)
    for j in range(out_ref.shape[0]):
        out_ref[j, :tokens, :] = attended
        out_ref[j, tokens:, :] = wout_ref[:, j * width:(j + 1) * width]


def attention(cache_len, query, key_new, value_new, cache_kv, w_out, groups):
    whole = lambda shape: pl.BlockSpec(shape, lambda i: (0,) * len(shape))
    tokens, width = query.shape
    packed_shape = (groups, tokens + w_out.shape[0], width)
    return pl.pallas_call(
        attention_kernel,
        grid=(1,),
        in_specs=[
            pl.BlockSpec(memory_space=pltpu.SMEM),
            whole(query.shape),
            whole(key_new.shape),
            whole(value_new.shape),
            whole(cache_kv.shape),
            whole(w_out.shape),
        ],
        out_specs=whole(packed_shape),
        out_shape=jax.ShapeDtypeStruct(packed_shape, jnp.bfloat16),
    )(cache_len, query, key_new, value_new, cache_kv, w_out)


def ffn_kernel(x_ref, gain_ref, gu_ref, down_ref, out_ref):
    groups, rows, width = x_ref.shape
    squares = jnp.zeros((rows, 1), jnp.float32)
    for g in range(groups):
        wide = x_ref[g].astype(jnp.float32)
        squares = squares + jnp.sum(wide * wide, axis=1, keepdims=True)
    inverse = lax.rsqrt(squares / D + EPS)
    gate = jnp.zeros((rows, gu_ref.shape[1]), jnp.float32)
    up = jnp.zeros((rows, gu_ref.shape[1]), jnp.float32)
    contract_last = (((1,), (1,)), ((), ()))
    for g in range(groups):
        x = (x_ref[g].astype(jnp.float32) * inverse * gain_ref[g:g + 1, :]).astype(jnp.bfloat16)
        gate = gate + lax.dot_general(
            x, gu_ref[0, :, g * width:(g + 1) * width], contract_last,
            preferred_element_type=jnp.float32,
        )
        up = up + lax.dot_general(
            x, gu_ref[1, :, g * width:(g + 1) * width], contract_last,
            preferred_element_type=jnp.float32,
        )
    hidden = (jax.nn.silu(gate) * up).astype(jnp.bfloat16)
    for g in range(groups):
        out_ref[g] = jnp.dot(
            hidden, down_ref[:, g * width:(g + 1) * width], preferred_element_type=jnp.float32
        ).astype(out_ref.dtype)


def expert_ffn(gathered, gain_blocks, gate_up, down, row_tile=512):
    groups, rows, width = gathered.shape
    return pl.pallas_call(
        ffn_kernel,
        grid=(rows // row_tile,),
        in_specs=[
            pl.BlockSpec((groups, row_tile, width), lambda i: (0, i, 0)),
            pl.BlockSpec(gain_blocks.shape, lambda i: (0, 0)),
            pl.BlockSpec(gate_up.shape, lambda i: (0, 0, 0)),
            pl.BlockSpec(down.shape, lambda i: (0, 0)),
        ],
        out_specs=pl.BlockSpec((groups, row_tile, width), lambda i: (0, i, 0)),
        out_shape=jax.ShapeDtypeStruct(gathered.shape, jnp.bfloat16),
    )(gathered, gain_blocks, gate_up, down)


def body(
    resid,
    query,
    key_new,
    value_new,
    cache_kv,
    cache_len,
    w_out,
    norm_gain,
    w_router,
    routes,
    w_gate_up,
    w_down,
):
    tokens_here = query.shape[0]
    heads_here = query.shape[1] // HD
    experts_all = w_router.shape[1]
    column_width = resid.shape[1]
    group_index = lax.axis_index("grp")
    request = lax.axis_index("ep")
    capacity = max(2, 8 * tokens_here // lax.axis_size("ep"))
    score_scale = float(HD) ** (-0.5)
    column_start = group_index * column_width
    groups = lax.axis_size("grp")
    packed = attention(cache_len, query, key_new, value_new, cache_kv, w_out, groups)
    packed = lax.all_to_all(packed, "grp", split_axis=0, concat_axis=0, tiled=True)
    attended_all = packed[:, :tokens_here, :]
    out_cols = packed[:, tokens_here:, :]
    attn_share = jnp.einsum(
        "gtd,gdc->tc",
        attended_all,
        out_cols.reshape(groups, column_width, column_width),
        preferred_element_type=jnp.float32,
    )
    after_cols = (resid.astype(jnp.float32) + attn_share).astype(jnp.bfloat16)
    after_full = lax.all_gather(after_cols, "grp", axis=1, tiled=True)
    after_wide = after_full.astype(jnp.float32)
    squares = jnp.sum(after_wide * after_wide, axis=1)
    inverse = lax.rsqrt(squares / D + EPS)
    normed_full = (
        after_wide * inverse[:, None] * norm_gain.astype(jnp.float32)[None, :]
    ).astype(jnp.bfloat16)
    logits = jnp.dot(normed_full, w_router, preferred_element_type=jnp.float32)
    route_hits = routes[:, :, None] == jnp.arange(experts_all, dtype=jnp.int32)[None, None, :]
    chosen = jnp.sum(jnp.where(route_hits, logits[:, None, :], 0.0), axis=-1)
    route_weight = jax.nn.softmax(chosen, axis=-1).astype(jnp.bfloat16)
    flat_hits = route_hits.reshape(tokens_here * TOP, experts_all).astype(jnp.int32)
    pair_ids = jnp.arange(tokens_here * TOP, dtype=jnp.int32)
    before = (pair_ids[None, :] < pair_ids[:, None]).astype(jnp.bfloat16)
    earlier = jnp.dot(before, flat_hits.astype(jnp.bfloat16), preferred_element_type=jnp.float32)
    slot_index = jnp.sum(earlier * flat_hits.astype(jnp.float32), axis=1).astype(jnp.int32)
    slot_row = (routes.reshape(-1) * capacity + slot_index).reshape(tokens_here, TOP)
    slot_ids = jnp.arange(experts_all * capacity, dtype=jnp.int32)
    matches = slot_row[:, :, None] == slot_ids[None, None, :]
    selection = jnp.any(matches, axis=1).astype(jnp.bfloat16)
    combine = jnp.sum(
        jnp.where(matches, route_weight[:, :, None].astype(jnp.float32), 0.0), axis=1
    )
    outgoing = jnp.einsum(
        "tj,td->jd", selection, after_cols, preferred_element_type=jnp.float32
    ).astype(jnp.bfloat16)
    outgoing = outgoing.reshape(experts_all, capacity, column_width)
    arrived = lax.all_to_all(outgoing, "ep", split_axis=0, concat_axis=0, tiled=True)
    arrived = arrived.reshape(experts_all * capacity, column_width)
    gathered = lax.all_gather(arrived, "grp", axis=0, tiled=False)
    gain_blocks = norm_gain.astype(jnp.float32).reshape(groups, column_width)
    slice_out = expert_ffn(gathered, gain_blocks, jnp.swapaxes(w_gate_up[0], 1, 2), w_down[0])
    expert_out = lax.psum_scatter(slice_out, "grp", scatter_dimension=0, tiled=True)
    expert_out = expert_out.reshape(experts_all, capacity, column_width)
    returned = lax.all_to_all(expert_out, "ep", split_axis=0, concat_axis=0, tiled=True)
    mixed_cols = jnp.dot(
        combine,
        returned.reshape(experts_all * capacity, column_width),
        precision=lax.Precision.HIGHEST,
        preferred_element_type=jnp.float32,
    )
    return (after_cols, mixed_cols.astype(jnp.bfloat16))


def solution(mesh):
    return jax.shard_map(
        body,
        mesh=mesh,
        in_specs=(
            P("ep", "grp"),
            P("ep", "grp"),
            P("ep", "grp"),
            P("ep", "grp"),
            P(None, "ep", "grp"),
            P(),
            P("grp", None),
            P(),
            P(),
            P("ep", None),
            P("ep", None, None, "grp"),
            P("ep", "grp", None),
        ),
        out_specs=(P("ep", "grp"), P("ep", "grp")),
        check_vma=False,
    )
```

```python
import jax
import jax.numpy as jnp
from jax import lax
from jax.experimental import pallas as pl
from jax.experimental.pallas import tpu as pltpu
from jax.sharding import PartitionSpec as P

D = 2048
HD = 128
TOP = 4


EPS = 1e-06
MASKED = -1e30


def attention_kernel(len_ref, q_ref, kn_ref, vn_ref, cache_ref, wout_ref, out_ref):
    tokens, width = q_ref.shape
    cache_rows = cache_ref.shape[1]
    length = len_ref[lax.axis_index("ep")]
    score_scale = float(HD) ** (-0.5)
    contract_last = (((1,), (1,)), ((), ()))
    causal = lax.broadcasted_iota(jnp.int32, (tokens, tokens), 0) >= lax.broadcasted_iota(
        jnp.int32, (tokens, tokens), 1
    )
    live = lax.broadcasted_iota(jnp.int32, (tokens, cache_rows), 1) < length
    heads = []
    for h in range(width // HD):
        cols = slice(h * HD, (h + 1) * HD)
        q = q_ref[:, cols]
        new_scores = (
            lax.dot_general(q, kn_ref[:, cols], contract_last, preferred_element_type=jnp.float32)
            * score_scale
        )
        new_scores = jnp.where(causal, new_scores, MASKED)
        old_scores = (
            lax.dot_general(
                q, cache_ref[0, :, cols], contract_last, preferred_element_type=jnp.float32
            )
            * score_scale
        )
        old_scores = jnp.where(live, old_scores, MASKED)
        row_max = jnp.maximum(
            jnp.max(new_scores, axis=1, keepdims=True), jnp.max(old_scores, axis=1, keepdims=True)
        )
        new_probs = jnp.exp(new_scores - row_max)
        old_probs = jnp.exp(old_scores - row_max)
        denominator = jnp.sum(new_probs, axis=1, keepdims=True) + jnp.sum(
            old_probs, axis=1, keepdims=True
        )
        weighted = jnp.dot(
            new_probs.astype(jnp.bfloat16), vn_ref[:, cols], preferred_element_type=jnp.float32
        ) + jnp.dot(
            old_probs.astype(jnp.bfloat16), cache_ref[1, :, cols], preferred_element_type=jnp.float32
        )
        heads.append((weighted / denominator).astype(jnp.bfloat16))
    attended = jnp.concatenate(heads, axis=1)
    for j in range(out_ref.shape[0]):
        out_ref[j, :tokens, :] = attended
        out_ref[j, tokens:, :] = wout_ref[:, j * width:(j + 1) * width]


def attention(cache_len, query, key_new, value_new, cache_kv, w_out, groups):
    whole = lambda shape: pl.BlockSpec(shape, lambda i: (0,) * len(shape))
    tokens, width = query.shape
    packed_shape = (groups, tokens + w_out.shape[0], width)
    return pl.pallas_call(
        attention_kernel,
        grid=(1,),
        in_specs=[
            pl.BlockSpec(memory_space=pltpu.SMEM),
            whole(query.shape),
            whole(key_new.shape),
            whole(value_new.shape),
            whole(cache_kv.shape),
            whole(w_out.shape),
        ],
        out_specs=whole(packed_shape),
        out_shape=jax.ShapeDtypeStruct(packed_shape, jnp.bfloat16),
    )(cache_len, query, key_new, value_new, cache_kv, w_out)


def ffn_kernel(x_ref, gain_ref, gu_ref, down_ref, out_ref):
    groups, rows, width = x_ref.shape
    squares = jnp.zeros((rows, 1), jnp.float32)
    for g in range(groups):
        wide = x_ref[g].astype(jnp.float32)
        squares = squares + jnp.sum(wide * wide, axis=1, keepdims=True)
    inverse = lax.rsqrt(squares / D + EPS)
    gate = jnp.zeros((rows, gu_ref.shape[1]), jnp.float32)
    up = jnp.zeros((rows, gu_ref.shape[1]), jnp.float32)
    contract_last = (((1,), (1,)), ((), ()))
    for g in range(groups):
        x = (x_ref[g].astype(jnp.float32) * inverse * gain_ref[g:g + 1, :]).astype(jnp.bfloat16)
        gate = gate + lax.dot_general(
            x, gu_ref[0, :, g * width:(g + 1) * width], contract_last,
            preferred_element_type=jnp.float32,
        )
        up = up + lax.dot_general(
            x, gu_ref[1, :, g * width:(g + 1) * width], contract_last,
            preferred_element_type=jnp.float32,
        )
    hidden = (jax.nn.silu(gate) * up).astype(jnp.bfloat16)
    for g in range(groups):
        out_ref[g] = jnp.dot(
            hidden, down_ref[:, g * width:(g + 1) * width], preferred_element_type=jnp.float32
        ).astype(out_ref.dtype)


def expert_ffn(gathered, gain_blocks, gate_up, down, row_tile=1024):
    groups, rows, width = gathered.shape
    return pl.pallas_call(
        ffn_kernel,
        grid=(rows // row_tile,),
        in_specs=[
            pl.BlockSpec((groups, row_tile, width), lambda i: (0, i, 0)),
            pl.BlockSpec(gain_blocks.shape, lambda i: (0, 0)),
            pl.BlockSpec(gate_up.shape, lambda i: (0, 0, 0)),
            pl.BlockSpec(down.shape, lambda i: (0, 0)),
        ],
        out_specs=pl.BlockSpec((groups, row_tile, width), lambda i: (0, i, 0)),
        out_shape=jax.ShapeDtypeStruct(gathered.shape, jnp.bfloat16),
    )(gathered, gain_blocks, gate_up, down)


def body(
    resid,
    query,
    key_new,
    value_new,
    cache_kv,
    cache_len,
    w_out,
    norm_gain,
    w_router,
    routes,
    w_gate_up,
    w_down,
):
    tokens_here = query.shape[0]
    heads_here = query.shape[1] // HD
    experts_all = w_router.shape[1]
    column_width = resid.shape[1]
    group_index = lax.axis_index("grp")
    request = lax.axis_index("ep")
    capacity = max(2, 8 * tokens_here // lax.axis_size("ep"))
    score_scale = float(HD) ** (-0.5)
    column_start = group_index * column_width
    groups = lax.axis_size("grp")
    packed = attention(cache_len, query, key_new, value_new, cache_kv, w_out, groups)
    packed = lax.all_to_all(packed, "grp", split_axis=0, concat_axis=0, tiled=True)
    attended_all = packed[:, :tokens_here, :]
    out_cols = packed[:, tokens_here:, :]
    attn_share = jnp.einsum(
        "gtd,gdc->tc",
        attended_all,
        out_cols.reshape(groups, column_width, column_width),
        preferred_element_type=jnp.float32,
    )
    after_cols = (resid.astype(jnp.float32) + attn_share).astype(jnp.bfloat16)
    after_full = lax.all_gather(after_cols, "grp", axis=1, tiled=True)
    after_wide = after_full.astype(jnp.float32)
    squares = jnp.sum(after_wide * after_wide, axis=1)
    inverse = lax.rsqrt(squares / D + EPS)
    normed_full = (
        after_wide * inverse[:, None] * norm_gain.astype(jnp.float32)[None, :]
    ).astype(jnp.bfloat16)
    logits = jnp.dot(normed_full, w_router, preferred_element_type=jnp.float32)
    route_hits = routes[:, :, None] == jnp.arange(experts_all, dtype=jnp.int32)[None, None, :]
    chosen = jnp.sum(jnp.where(route_hits, logits[:, None, :], 0.0), axis=-1)
    route_weight = jax.nn.softmax(chosen, axis=-1).astype(jnp.bfloat16)
    flat_hits = route_hits.reshape(tokens_here * TOP, experts_all).astype(jnp.int32)
    pair_ids = jnp.arange(tokens_here * TOP, dtype=jnp.int32)
    before = (pair_ids[None, :] < pair_ids[:, None]).astype(jnp.bfloat16)
    earlier = jnp.dot(before, flat_hits.astype(jnp.bfloat16), preferred_element_type=jnp.float32)
    slot_index = jnp.sum(earlier * flat_hits.astype(jnp.float32), axis=1).astype(jnp.int32)
    slot_row = (routes.reshape(-1) * capacity + slot_index).reshape(tokens_here, TOP)
    slot_ids = jnp.arange(experts_all * capacity, dtype=jnp.int32)
    matches = slot_row[:, :, None] == slot_ids[None, None, :]
    selection = jnp.any(matches, axis=1).astype(jnp.bfloat16)
    combine = jnp.sum(
        jnp.where(matches, route_weight[:, :, None].astype(jnp.float32), 0.0), axis=1
    )
    outgoing = jnp.einsum(
        "tj,td->jd", selection, after_cols, preferred_element_type=jnp.float32
    ).astype(jnp.bfloat16)
    outgoing = outgoing.reshape(experts_all, capacity, column_width)
    arrived = lax.all_to_all(outgoing, "ep", split_axis=0, concat_axis=0, tiled=True)
    arrived = arrived.reshape(experts_all * capacity, column_width)
    gathered = lax.all_gather(arrived, "grp", axis=0, tiled=False)
    gain_blocks = norm_gain.astype(jnp.float32).reshape(groups, column_width)
    slice_out = expert_ffn(gathered, gain_blocks, jnp.swapaxes(w_gate_up[0], 1, 2), w_down[0])
    expert_out = lax.psum_scatter(slice_out, "grp", scatter_dimension=0, tiled=True)
    expert_out = expert_out.reshape(experts_all, capacity, column_width)
    returned = lax.all_to_all(expert_out, "ep", split_axis=0, concat_axis=0, tiled=True)
    mixed_cols = jnp.dot(
        combine,
        returned.reshape(experts_all * capacity, column_width),
        precision=lax.Precision.HIGHEST,
        preferred_element_type=jnp.float32,
    )
    return (after_cols, mixed_cols.astype(jnp.bfloat16))


def solution(mesh):
    return jax.shard_map(
        body,
        mesh=mesh,
        in_specs=(
            P("ep", "grp"),
            P("ep", "grp"),
            P("ep", "grp"),
            P("ep", "grp"),
            P(None, "ep", "grp"),
            P(),
            P("grp", None),
            P(),
            P(),
            P("ep", None),
            P("ep", None, None, "grp"),
            P("ep", "grp", None),
        ),
        out_specs=(P("ep", "grp"), P("ep", "grp")),
        check_vma=False,
    )
```

```python
import jax
import jax.numpy as jnp
from jax import lax
from jax.experimental import pallas as pl
from jax.experimental.pallas import tpu as pltpu
from jax.sharding import PartitionSpec as P

D = 2048
HD = 128
TOP = 4


EPS = 1e-06
MASKED = -1e30


def attention_kernel(len_ref, q_ref, kn_ref, vn_ref, cache_ref, wout_ref, out_ref):
    tokens, width = q_ref.shape
    cache_rows = cache_ref.shape[1]
    length = len_ref[lax.axis_index("ep")]
    score_scale = float(HD) ** (-0.5)
    contract_last = (((1,), (1,)), ((), ()))
    causal = lax.broadcasted_iota(jnp.int32, (tokens, tokens), 0) >= lax.broadcasted_iota(
        jnp.int32, (tokens, tokens), 1
    )
    live = lax.broadcasted_iota(jnp.int32, (tokens, cache_rows), 1) < length
    heads = []
    for h in range(width // HD):
        cols = slice(h * HD, (h + 1) * HD)
        q = q_ref[:, cols]
        new_scores = (
            lax.dot_general(q, kn_ref[:, cols], contract_last, preferred_element_type=jnp.float32)
            * score_scale
        )
        new_scores = jnp.where(causal, new_scores, MASKED)
        old_scores = (
            lax.dot_general(
                q, cache_ref[0, :, cols], contract_last, preferred_element_type=jnp.float32
            )
            * score_scale
        )
        old_scores = jnp.where(live, old_scores, MASKED)
        row_max = jnp.maximum(
            jnp.max(new_scores, axis=1, keepdims=True), jnp.max(old_scores, axis=1, keepdims=True)
        )
        new_probs = jnp.exp(new_scores - row_max)
        old_probs = jnp.exp(old_scores - row_max)
        denominator = jnp.sum(new_probs, axis=1, keepdims=True) + jnp.sum(
            old_probs, axis=1, keepdims=True
        )
        weighted = jnp.dot(
            new_probs.astype(jnp.bfloat16), vn_ref[:, cols], preferred_element_type=jnp.float32
        ) + jnp.dot(
            old_probs.astype(jnp.bfloat16), cache_ref[1, :, cols], preferred_element_type=jnp.float32
        )
        heads.append((weighted / denominator).astype(jnp.bfloat16))
    attended = jnp.concatenate(heads, axis=1)
    for j in range(out_ref.shape[0]):
        out_ref[j, :tokens, :] = attended
        out_ref[j, tokens:, :] = wout_ref[:, j * width:(j + 1) * width]


def attention(cache_len, query, key_new, value_new, cache_kv, w_out, groups):
    whole = lambda shape: pl.BlockSpec(shape, lambda i: (0,) * len(shape))
    tokens, width = query.shape
    packed_shape = (groups, tokens + w_out.shape[0], width)
    return pl.pallas_call(
        attention_kernel,
        grid=(1,),
        in_specs=[
            pl.BlockSpec(memory_space=pltpu.SMEM),
            whole(query.shape),
            whole(key_new.shape),
            whole(value_new.shape),
            whole(cache_kv.shape),
            whole(w_out.shape),
        ],
        out_specs=whole(packed_shape),
        out_shape=jax.ShapeDtypeStruct(packed_shape, jnp.bfloat16),
    )(cache_len, query, key_new, value_new, cache_kv, w_out)


def ffn_kernel(x_ref, gain_ref, gu_ref, down_ref, out_ref):
    groups, rows, width = x_ref.shape
    squares = jnp.zeros((rows, 1), jnp.float32)
    for g in range(groups):
        wide = x_ref[g].astype(jnp.float32)
        squares = squares + jnp.sum(wide * wide, axis=1, keepdims=True)
    inverse = lax.rsqrt(squares / D + EPS)
    gate = jnp.zeros((rows, gu_ref.shape[1]), jnp.float32)
    up = jnp.zeros((rows, gu_ref.shape[1]), jnp.float32)
    contract_last = (((1,), (1,)), ((), ()))
    for g in range(groups):
        x = (x_ref[g].astype(jnp.float32) * inverse * gain_ref[g:g + 1, :]).astype(jnp.bfloat16)
        gate = gate + lax.dot_general(
            x, gu_ref[0, :, g * width:(g + 1) * width], contract_last,
            preferred_element_type=jnp.float32,
        )
        up = up + lax.dot_general(
            x, gu_ref[1, :, g * width:(g + 1) * width], contract_last,
            preferred_element_type=jnp.float32,
        )
    hidden = (jax.nn.silu(gate) * up).astype(jnp.bfloat16)
    for g in range(groups):
        out_ref[g] = jnp.dot(
            hidden, down_ref[:, g * width:(g + 1) * width], preferred_element_type=jnp.float32
        ).astype(out_ref.dtype)


def expert_ffn(gathered, gain_blocks, gate_up, down, row_tile=512):
    groups, rows, width = gathered.shape
    return pl.pallas_call(
        ffn_kernel,
        grid=(rows // row_tile,),
        in_specs=[
            pl.BlockSpec((groups, row_tile, width), lambda i: (0, i, 0)),
            pl.BlockSpec(gain_blocks.shape, lambda i: (0, 0)),
            pl.BlockSpec(gate_up.shape, lambda i: (0, 0, 0)),
            pl.BlockSpec(down.shape, lambda i: (0, 0)),
        ],
        out_specs=pl.BlockSpec((groups, row_tile, width), lambda i: (0, i, 0)),
        out_shape=jax.ShapeDtypeStruct(gathered.shape, jnp.bfloat16),
    )(gathered, gain_blocks, gate_up, down)


def body(
    resid,
    query,
    key_new,
    value_new,
    cache_kv,
    cache_len,
    w_out,
    norm_gain,
    w_router,
    routes,
    w_gate_up,
    w_down,
):
    tokens_here = query.shape[0]
    heads_here = query.shape[1] // HD
    experts_all = w_router.shape[1]
    column_width = resid.shape[1]
    group_index = lax.axis_index("grp")
    request = lax.axis_index("ep")
    capacity = max(2, 8 * tokens_here // lax.axis_size("ep"))
    score_scale = float(HD) ** (-0.5)
    column_start = group_index * column_width
    groups = lax.axis_size("grp")
    packed = attention(cache_len, query, key_new, value_new, cache_kv, w_out, groups)
    packed = lax.all_to_all(packed, "grp", split_axis=0, concat_axis=0, tiled=True)
    attended_all = packed[:, :tokens_here, :]
    out_cols = packed[:, tokens_here:, :]
    attn_share = jnp.einsum(
        "gtd,gdc->tc",
        attended_all,
        out_cols.reshape(groups, column_width, column_width),
        preferred_element_type=jnp.float32,
    )
    after_cols = (resid.astype(jnp.float32) + attn_share).astype(jnp.bfloat16)
    after_full = lax.all_gather(after_cols, "grp", axis=1, tiled=True)
    after_wide = after_full.astype(jnp.float32)
    squares = jnp.sum(after_wide * after_wide, axis=1)
    inverse = lax.rsqrt(squares / D + EPS)
    normed_full = (
        after_wide * inverse[:, None] * norm_gain.astype(jnp.float32)[None, :]
    ).astype(jnp.bfloat16)
    logits = jnp.dot(normed_full, w_router, preferred_element_type=jnp.float32)
    route_hits = routes[:, :, None] == jnp.arange(experts_all, dtype=jnp.int32)[None, None, :]
    chosen = jnp.sum(jnp.where(route_hits, logits[:, None, :], 0.0), axis=-1)
    route_weight = jax.nn.softmax(chosen, axis=-1).astype(jnp.bfloat16)
    flat_hits = route_hits.reshape(tokens_here * TOP, experts_all).astype(jnp.int32)
    pair_ids = jnp.arange(tokens_here * TOP, dtype=jnp.int32)
    before = (pair_ids[None, :] < pair_ids[:, None]).astype(jnp.bfloat16)
    earlier = jnp.dot(before, flat_hits.astype(jnp.bfloat16), preferred_element_type=jnp.float32)
    slot_index = jnp.sum(earlier * flat_hits.astype(jnp.float32), axis=1).astype(jnp.int32)
    slot_row = (routes.reshape(-1) * capacity + slot_index).reshape(tokens_here, TOP)
    slot_ids = jnp.arange(experts_all * capacity, dtype=jnp.int32)
    matches = slot_row[:, :, None] == slot_ids[None, None, :]
    selection = jnp.any(matches, axis=1).astype(jnp.bfloat16)
    combine = jnp.sum(
        jnp.where(matches, route_weight[:, :, None].astype(jnp.float32), 0.0), axis=1
    )
    outgoing = jnp.einsum("tj,td->jd", selection, after_cols, preferred_element_type=jnp.bfloat16)
    outgoing = outgoing.reshape(experts_all, capacity, column_width)
    arrived = lax.all_to_all(outgoing, "ep", split_axis=0, concat_axis=0, tiled=True)
    arrived = arrived.reshape(experts_all * capacity, column_width)
    gathered = lax.all_gather(arrived, "grp", axis=0, tiled=False)
    gain_blocks = norm_gain.astype(jnp.float32).reshape(groups, column_width)
    slice_out = expert_ffn(gathered, gain_blocks, jnp.swapaxes(w_gate_up[0], 1, 2), w_down[0])
    expert_out = lax.psum_scatter(slice_out, "grp", scatter_dimension=0, tiled=True)
    expert_out = expert_out.reshape(experts_all, capacity, column_width)
    returned = lax.all_to_all(expert_out, "ep", split_axis=0, concat_axis=0, tiled=True)
    mixed_cols = jnp.dot(
        combine,
        returned.reshape(experts_all * capacity, column_width),
        precision=lax.Precision.HIGHEST,
        preferred_element_type=jnp.float32,
    )
    return (after_cols, mixed_cols.astype(jnp.bfloat16))


def solution(mesh):
    return jax.shard_map(
        body,
        mesh=mesh,
        in_specs=(
            P("ep", "grp"),
            P("ep", "grp"),
            P("ep", "grp"),
            P("ep", "grp"),
            P(None, "ep", "grp"),
            P(),
            P("grp", None),
            P(),
            P(),
            P("ep", None),
            P("ep", None, None, "grp"),
            P("ep", "grp", None),
        ),
        out_specs=(P("ep", "grp"), P("ep", "grp")),
        check_vma=False,
    )
```
